32 devices in a mesh: head: 2 (over y), ctx: 4 (over z), batch: 4 (over x, core).
Axes of the slice: x: 2, y: 2, z: 4, core: 2. Of those that a mesh axis runs over, the one named last changes fastest.
Arguments:
- tokens: bfloat16 [4, 1024, 1024], P('batch', ('ctx', 'head')), may hold values from -6 to 6
- cotangent: bfloat16 [4, 1024, 1024], P('batch', ('ctx', 'head')), may hold values from -6 to 6
- norm1_gain: bfloat16 [1024], P(('head', 'ctx', 'batch')), may hold values from 0.5 to 1.5
- w_query: bfloat16 [1024, 1024], P(('head', 'ctx', 'batch')), may hold values from -0.1875 to 0.1875
- w_key: bfloat16 [1024, 1024], P(('head', 'ctx', 'batch')), may hold values from -0.1875 to 0.1875
- w_value: bfloat16 [1024, 2048], P(('head', 'ctx', 'batch')), may hold values from -0.1875 to 0.1875
- w_gate: bfloat16 [1024, 2048], P(('head', 'ctx', 'batch')), may hold values from -0.1875 to 0.1875
- w_rates: bfloat16 [1024, 16], P(('head', 'ctx', 'batch')), may hold values from -0.1875 to 0.1875
- conv_query: bfloat16 [4, 1024], P(None, 'head'), may hold values from -3 to 3
- conv_key: bfloat16 [4, 1024], P(None, 'head'), may hold values from -3 to 3
- conv_value: bfloat16 [4, 2048], P(None, 'head'), may hold values from -3 to 3
- decay_log: float32 [8], P('head'), may hold values from -7 to 0.5
- decay_bias: float32 [8], P('head'), may hold values from -4 to 1
- out_gain: bfloat16 [2048], P('head'), may hold values from 0.5 to 1.5
- w_out: bfloat16 [1024, 2048], P(('head', 'ctx', 'batch')), may hold values from -0.125 to 0.125
- norm2_gain: bfloat16 [1024], P(('head', 'ctx', 'batch')), may hold values from 0.5 to 1.5
- w_ffgate: bfloat16 [1024, 2816], P(('head', 'ctx', 'batch')), may hold values from -0.1875 to 0.1875
- w_ffup: bfloat16 [1024, 2816], P(('head', 'ctx', 'batch')), may hold values from -0.1875 to 0.1875
- w_down: bfloat16 [1024, 2816], P(('head', 'ctx', 'batch')), may hold values from -0.109375 to 0.109375
Outputs:
- output: bfloat16 [4, 1024, 1024], P('batch', ('ctx', 'head'))
- input_grad: float32 [4, 1024, 1024], P('batch', ('ctx', 'head'))
- g_norm1: float32 [1024], P(('head', 'ctx', 'batch'))
- g_query: float32 [1024, 1024], P(('ctx', 'batch'), 'head')
- g_key: float32 [1024, 1024], P(('ctx', 'batch'), 'head')
- g_value: float32 [1024, 2048], P(('ctx', 'batch'), 'head')
- g_gate: float32 [1024, 2048], P(('ctx', 'batch'), 'head')
- g_rates: float32 [1024, 16], P(('ctx', 'batch'), 'head')
- g_conv_query: float32 [4, 1024], P(None, 'head')
- g_conv_key: float32 [4, 1024], P(None, 'head')
- g_conv_value: float32 [4, 2048], P(None, 'head')
- g_decay_log: float32 [8], P('head')
- g_decay_bias: float32 [8], P('head')
- g_out_gain: float32 [2048], P('head')
- g_out: float32 [1024, 2048], P(('ctx', 'batch'), 'head')
- g_norm2: float32 [1024], P(('head', 'ctx', 'batch'))
- g_ffgate: float32 [1024, 2816], P(('ctx', 'batch'), 'head')
- g_ffup: float32 [1024, 2816], P(('ctx', 'batch'), 'head')
- g_down: float32 [1024, 2816], P(('ctx', 'batch'), 'head')
The draws below stay inside these ranges and needn't reach their ends.
All inputs are finite; a program needn't handle non-finite values.
Results may differ from the reference program's by a relative error of at most 0.02.
Values may be sent and summed in bfloat16 or wider, within the bound.
A program may use at most 256 MiB of HBM per device.

```python
import math
import jax
import jax.numpy as jnp
from jax import lax

D = 1024
H = 8
DK = 128
DV = 256
FF = 2816
KW = 4
SPAN = 64
SEQS = 4
PIECE = 256
LENGTH = 1024
N_CTX = 4


def block_levels(rng, shape, pieces, least, largest):
    level = 1.0
    for axis_at, parts in pieces:
        draws = jax.random.uniform(jax.random.fold_in(jax.random.fold_in(rng, 6), axis_at), (parts,), jnp.float32, least / len(pieces), largest / len(pieces))
        level = level * jnp.repeat(jnp.exp(draws), shape[axis_at] // parts).reshape((-1,) + (1,) * (len(shape) - 1 - axis_at))
    return level


def gaussian(stream_key, extent, scale, bound, cuts=(), kind=jnp.bfloat16):
    drawn = jax.random.normal(stream_key, extent, jnp.float32) * scale
    if len(cuts) > 0:
        drawn = block_levels(stream_key, extent, cuts, -0.22, 0.18) * drawn
    return jnp.clip(drawn, min=-bound, max=bound).astype(kind)


def setup_inputs(seed: int = 0) -> dict:
    key_list = jax.random.split(jax.random.key(seed), 20)
    tokens = gaussian(key_list[0], (SEQS, LENGTH, D), 1.0, 6.0, ((0, 4), (1, 8)))
    cotangent = gaussian(key_list[1], (SEQS, LENGTH, D), 1.0, 6.0, ((0, 4), (1, 8)))
    norm1_gain = jnp.clip(1.0 + 0.1 * jax.random.normal(key_list[2], (D,), jnp.float32), 0.5, 1.5).astype(jnp.bfloat16)
    w_query = gaussian(key_list[3], (D, H * DK), D ** -0.5, 0.1875, ((0, 32),))
    w_key = gaussian(key_list[4], (D, H * DK), D ** -0.5, 0.1875, ((0, 32),))
    w_value = gaussian(key_list[5], (D, H * DV), D ** -0.5, 0.1875, ((0, 32),))
    w_gate = gaussian(key_list[6], (D, H * DV), D ** -0.5, 0.1875, ((0, 32),))
    w_rates = gaussian(key_list[7], (D, 2 * H), D ** -0.5, 0.1875, ((0, 32),))
    conv_query = gaussian(key_list[8], (KW, H * DK), KW ** -0.5, 3.0, ((1, 2),))
    conv_key = gaussian(key_list[9], (KW, H * DK), KW ** -0.5, 3.0, ((1, 2),))
    conv_value = gaussian(key_list[10], (KW, H * DV), KW ** -0.5, 3.0, ((1, 2),))
    decay_log = jnp.clip(-7.0 + 7.5 * jax.random.uniform(key_list[11], (H,), jnp.float32) ** block_levels(key_list[11], (H,), ((0, 2),), -0.2, 0.2), -7.0, 0.5)
    decay_bias = jnp.clip(-4.0 + 5.0 * jax.random.uniform(key_list[12], (H,), jnp.float32) ** block_levels(key_list[12], (H,), ((0, 2),), -0.2, 0.2), -4.0, 1.0)
    out_gain = jnp.clip(1.0 + 0.1 * jax.random.normal(key_list[13], (H * DV,), jnp.float32), 0.5, 1.5).astype(jnp.bfloat16)
    w_out = gaussian(key_list[14], (D, H * DV), (H * DV) ** -0.5, 0.125, ((0, 32),))
    norm2_gain = jnp.clip(1.0 + 0.1 * jax.random.normal(key_list[15], (D,), jnp.float32), 0.5, 1.5).astype(jnp.bfloat16)
    w_ffgate = gaussian(key_list[16], (D, FF), D ** -0.5, 0.1875, ((0, 32),))
    w_ffup = gaussian(key_list[17], (D, FF), D ** -0.5, 0.1875, ((0, 32),))
    w_down = gaussian(key_list[18], (D, FF), FF ** -0.5, 0.109375, ((0, 32),))
    return {"tokens": tokens, "cotangent": cotangent, "norm1_gain": norm1_gain, "w_query": w_query, "w_key": w_key, "w_value": w_value, "w_gate": w_gate, "w_rates": w_rates, "conv_query": conv_query, "conv_key": conv_key, "conv_value": conv_value, "decay_log": decay_log, "decay_bias": decay_bias, "out_gain": out_gain, "w_out": w_out, "norm2_gain": norm2_gain, "w_ffgate": w_ffgate, "w_ffup": w_ffup, "w_down": w_down}


epsilon = 1e-06
highest_precision = lax.Precision.HIGHEST

def mat_nt(first_mat, second_mat):
    return lax.dot_general(first_mat.astype(jnp.float32), second_mat.astype(jnp.float32), (((1,), (1,)), ((), ())), preferred_element_type=jnp.float32)

def mat_tn(first_mat, second_mat):
    return lax.dot_general(first_mat.astype(jnp.float32), second_mat.astype(jnp.float32), (((0,), (0,)), ((), ())), preferred_element_type=jnp.float32)

def piece_total(left_rows, right_rows):
    left_pieces = left_rows.reshape(N_CTX, PIECE, left_rows.shape[1])
    right_pieces = right_rows.reshape(N_CTX, PIECE, right_rows.shape[1])

    def add_piece(running, operands):
        rounded = lax.optimization_barrier(mat_tn(operands[0], operands[1]).astype(jnp.bfloat16))
        return (running + rounded.astype(jnp.float32), None)
    start_sum = jnp.zeros((left_rows.shape[1], right_rows.shape[1]), jnp.float32)
    running, unused_rows = lax.scan(add_piece, start_sum, (left_pieces, right_pieces))
    return running

def rms_scale(hidden, gain_vec):
    return hidden * lax.rsqrt(lax.optimization_barrier(jnp.mean(hidden * hidden, axis=-1, keepdims=True)) + epsilon) * gain_vec

def swiglu(gate_part, up_part):
    return jax.nn.silu(gate_part) * up_part

def unit_rows(matrix):
    return matrix * lax.rsqrt(lax.optimization_barrier(jnp.sum(matrix * matrix, axis=-1, keepdims=True)) + epsilon)

def prepare(padded, conv_all, rates, decay_log, decay_bias):
    head_count = decay_log.shape[0]
    length = padded.shape[0] - (KW - 1)
    mixed_rows = padded[0:length] * conv_all[0]
    for tap_index in range(1, KW):
        mixed_rows = mixed_rows + padded[tap_index:tap_index + length] * conv_all[tap_index]
    active = jax.nn.silu(mixed_rows)
    split_one = head_count * DK
    queries = unit_rows(active[:, :split_one].reshape(length, head_count, DK)) / math.sqrt(DK)
    keys_vec = unit_rows(active[:, split_one:2 * split_one].reshape(length, head_count, DK))
    values = active[:, 2 * split_one:].reshape(length, head_count, DV)
    rate_pairs = rates.reshape(length, head_count, 2)
    log_decay = -jnp.exp(decay_log) * jax.nn.softplus(rate_pairs[:, :, 0] + decay_bias)
    strength = jax.nn.sigmoid(rate_pairs[:, :, 1])
    return (queries, keys_vec, values, log_decay, strength)

def span_parts(keys_blk, values_blk, decay_blk, strength_blk):
    key_heads = jnp.transpose(keys_blk, (1, 0, 2))
    value_heads = jnp.transpose(values_blk, (1, 0, 2))
    cumulative = jnp.cumsum(jnp.transpose(decay_blk), axis=1)
    strength_heads = jnp.transpose(strength_blk)
    block_size = cumulative.shape[1]
    row_index = jnp.arange(block_size)[:, None]
    col_index = jnp.arange(block_size)[None, :]
    strict = row_index > col_index
    inclusive = row_index >= col_index
    gaps = cumulative[:, :, None] - cumulative[:, None, :]
    below_decay = jnp.where(strict, jnp.exp(jnp.where(strict, gaps, 0.0)), 0.0)
    key_gram = jnp.einsum('htd,hsd->hts', key_heads, key_heads, precision=highest_precision)
    system = jnp.eye(block_size, dtype=jnp.float32) + strength_heads[:, :, None] * below_decay * key_gram
    decay_factor = jnp.exp(cumulative)
    targets = jnp.concatenate([strength_heads[:, :, None] * value_heads, (strength_heads * decay_factor)[:, :, None] * key_heads], axis=2)
    solved = jax.scipy.linalg.solve_triangular(system, targets, lower=True, unit_diagonal=True)
    value_width = value_heads.shape[2]
    direct_term = solved[:, :, :value_width]
    across_devices_total = solved[:, :, value_width:]
    tail_decay = jnp.exp(cumulative[:, -1:] - cumulative)
    decayed_key_rows = tail_decay[:, :, None] * key_heads
    final_decay_factor = jnp.exp(cumulative[:, -1])
    within = jnp.where(inclusive, jnp.exp(jnp.where(inclusive, gaps, 0.0)), 0.0)
    return (key_heads, decay_factor, within, direct_term, across_devices_total, decayed_key_rows, final_decay_factor)

def delta_block(incoming_state, block_in):
    query_blk, keys_blk, values_blk, decay_blk, strength_blk = block_in
    key_heads, decay_factor, within, direct_term, across_devices_total, decayed_key_rows, final_decay_factor = span_parts(keys_blk, values_blk, decay_blk, strength_blk)
    query_head_rows = jnp.transpose(query_blk, (1, 0, 2))
    state_update = direct_term - jnp.einsum('nal,nlr->nar', across_devices_total, incoming_state, precision=highest_precision)
    scores = jnp.einsum('htd,hsd->hts', query_head_rows, key_heads, precision=highest_precision) * within
    layer_result = decay_factor[:, :, None] * jnp.einsum('nal,nlr->nar', query_head_rows, incoming_state, precision=highest_precision)
    layer_result = layer_result + jnp.einsum('hts,hsv->htv', scores, state_update, precision=highest_precision)
    updated_state = final_decay_factor[:, None, None] * incoming_state + jnp.einsum('pex,ped->pxd', decayed_key_rows, state_update, precision=highest_precision)
    return (updated_state, jnp.transpose(layer_result, (1, 0, 2)))

def into_blocks(tensor):
    return tensor.reshape((tensor.shape[0] // SPAN, SPAN) + tensor.shape[1:])

def mixer_out(queries, keys_vec, values, log_decay, strength, initial_state):
    final_state, outputs = lax.scan(delta_block, initial_state, (into_blocks(queries), into_blocks(keys_vec), into_blocks(values), into_blocks(log_decay), into_blocks(strength)))
    return outputs.reshape((queries.shape[0],) + outputs.shape[2:])

def out_gate(mixer_rows, gate_rows, gain_vec):
    normed = mixer_rows * lax.rsqrt(lax.optimization_barrier(jnp.mean(mixer_rows * mixer_rows, axis=-1, keepdims=True)) + epsilon)
    flat = normed.reshape(mixer_rows.shape[0], mixer_rows.shape[1] * mixer_rows.shape[2])
    return flat * gain_vec * jax.nn.silu(gate_rows)

def one_sequence(seq_tokens, seq_cot, params):
    norm1_gain, w_query, w_key, w_value, w_gate, w_rates, conv_query, conv_key, conv_value, decay_log, decay_bias, out_gain, w_out, norm2_gain, w_ffgate, w_ffup, w_down = params
    residual = seq_tokens.astype(jnp.float32)
    normed_f, norm_one_vjp = jax.vjp(rms_scale, residual, norm1_gain.astype(jnp.float32))
    normed_one = normed_f.astype(jnp.bfloat16)
    query_raw = jnp.dot(normed_one.astype(jnp.float32), w_query.astype(jnp.float32), preferred_element_type=jnp.float32).astype(jnp.bfloat16)
    key_raw = jnp.dot(normed_one.astype(jnp.float32), w_key.astype(jnp.float32), preferred_element_type=jnp.float32).astype(jnp.bfloat16)
    value_raw = jnp.dot(normed_one.astype(jnp.float32), w_value.astype(jnp.float32), preferred_element_type=jnp.float32).astype(jnp.bfloat16)
    gate_raw = jnp.dot(normed_one.astype(jnp.float32), w_gate.astype(jnp.float32), preferred_element_type=jnp.float32).astype(jnp.bfloat16)
    rates_raw = jnp.dot(normed_one.astype(jnp.float32), w_rates.astype(jnp.float32), preferred_element_type=jnp.float32).astype(jnp.bfloat16)
    joined = jnp.concatenate([query_raw, key_raw, value_raw], axis=1).astype(jnp.float32)
    padded = jnp.concatenate([jnp.zeros((KW - 1, joined.shape[1]), jnp.float32), joined], axis=0)
    conv_all = jnp.concatenate([conv_query, conv_key, conv_value], axis=1).astype(jnp.float32)
    prepared, prepare_vjp = jax.vjp(prepare, padded, conv_all, rates_raw.astype(jnp.float32), decay_log, decay_bias)
    queries, keys_vec, values, log_decay, strength = prepared
    zero_state = jnp.zeros((H, DK, DV), jnp.float32)
    mixer_rows, mixer_vjp = jax.vjp(mixer_out, queries, keys_vec, values, log_decay, strength, zero_state)
    gated_f, gate_vjp = jax.vjp(out_gate, mixer_rows, gate_raw.astype(jnp.float32), out_gain.astype(jnp.float32))
    gated = gated_f.astype(jnp.bfloat16)
    middle = residual + mat_nt(gated, w_out)
    normed_two_f, norm_two_vjp = jax.vjp(rms_scale, middle, norm2_gain.astype(jnp.float32))
    normed_two = normed_two_f.astype(jnp.bfloat16)
    ff_gate = jnp.dot(normed_two.astype(jnp.float32), w_ffgate.astype(jnp.float32), preferred_element_type=jnp.float32)
    ff_up = jnp.dot(normed_two.astype(jnp.float32), w_ffup.astype(jnp.float32), preferred_element_type=jnp.float32)
    hidden_f, swiglu_vjp = jax.vjp(swiglu, ff_gate, ff_up)
    hidden = hidden_f.astype(jnp.bfloat16)
    output_seq = (middle + mat_nt(hidden, w_down)).astype(jnp.bfloat16)
    hidden_grad = jnp.dot(seq_cot.astype(jnp.float32), w_down.astype(jnp.float32), preferred_element_type=jnp.float32)
    gate_grad_f, up_grad_f = swiglu_vjp(hidden_grad)
    ffgate_grad = gate_grad_f.astype(jnp.bfloat16)
    ffup_grad = up_grad_f.astype(jnp.bfloat16)
    normed_two_grad = mat_nt(ffgate_grad, w_ffgate) + mat_nt(ffup_grad, w_ffup)
    middle_part, gain_two_grad = norm_two_vjp(normed_two_grad)
    middle_grad = seq_cot.astype(jnp.float32) + middle_part
    middle_grad_b = middle_grad.astype(jnp.bfloat16)
    gated_grad = jnp.dot(middle_grad_b.astype(jnp.float32), w_out.astype(jnp.float32), preferred_element_type=jnp.float32).astype(jnp.bfloat16)
    mixer_grad, gate_grad_f2, out_gain_grad = gate_vjp(gated_grad.astype(jnp.float32))
    query_g, key_g, value_g, decay_g, strength_g, unused_state = mixer_vjp(mixer_grad)
    padded_grad, conv_grad, rates_grad_f, decay_log_grad, decay_bias_grad = prepare_vjp((query_g, key_g, value_g, decay_g, strength_g))
    raw_grad = padded_grad[KW - 1:].astype(jnp.bfloat16)
    query_width = H * DK
    query_grad = raw_grad[:, :query_width]
    key_grad = raw_grad[:, query_width:2 * query_width]
    value_grad = raw_grad[:, 2 * query_width:]
    gate_grad = gate_grad_f2.astype(jnp.bfloat16)
    rates_grad = rates_grad_f.astype(jnp.bfloat16)
    normed_one_grad = mat_nt(query_grad, w_query) + mat_nt(key_grad, w_key) + mat_nt(value_grad, w_value) + mat_nt(gate_grad, w_gate) + mat_nt(rates_grad, w_rates)
    input_part, gain_one_grad = norm_one_vjp(normed_one_grad)
    input_grad = middle_grad + input_part
    grads = (gain_one_grad, piece_total(normed_one, query_grad), piece_total(normed_one, key_grad), piece_total(normed_one, value_grad), piece_total(normed_one, gate_grad), piece_total(normed_one, rates_grad), conv_grad[:, :query_width], conv_grad[:, query_width:2 * query_width], conv_grad[:, 2 * query_width:], decay_log_grad, decay_bias_grad, out_gain_grad, piece_total(middle_grad_b, gated), gain_two_grad, piece_total(normed_two, ffgate_grad), piece_total(normed_two, ffup_grad), piece_total(seq_cot, hidden))
    return (output_seq, input_grad, grads)

def reference(tokens, cotangent, norm1_gain, w_query, w_key, w_value, w_gate, w_rates, conv_query, conv_key, conv_value, decay_log, decay_bias, out_gain, w_out, norm2_gain, w_ffgate, w_ffup, w_down):
    params = (norm1_gain, w_query, w_key, w_value, w_gate, w_rates, conv_query, conv_key, conv_value, decay_log, decay_bias, out_gain, w_out, norm2_gain, w_ffgate, w_ffup, w_down)
    totals_init = tuple((jnp.zeros(param.shape, jnp.float32) for param in params))

    def per_sequence(totals, pair):
        output_seq, input_grad, grads = one_sequence(pair[0], pair[1], params)
        return (jax.tree.map(jnp.add, totals, grads), (output_seq, input_grad))
    totals, stacked = lax.scan(per_sequence, totals_init, (tokens, cotangent))
    return (stacked[0], stacked[1], totals[0], totals[1], totals[2], totals[3], totals[4], totals[5], totals[6], totals[7], totals[8], totals[9], totals[10], totals[11], totals[12], totals[13], totals[14], totals[15], totals[16])
```

```python
import functools
import math

import jax
import jax.numpy as jnp
from jax import lax
from jax.experimental import pallas as pl
from jax.experimental.pallas import tpu as pltpu
from jax.sharding import PartitionSpec as P

KW = 4
CHUNK = 256
epsilon = 1e-06
highest_precision = lax.Precision.HIGHEST


def passed_along(block, axis, distance):
    devices = range(lax.axis_size(axis))
    route = [(i - distance, i) for i in devices if i - distance in devices]
    return lax.ppermute(block, axis, route)


def halves(matrix):
    high = matrix.astype(jnp.bfloat16)
    return high, (matrix - high.astype(jnp.float32)).astype(jnp.bfloat16)


def one_pass(first, second, first_dim, second_dim):
    return lax.dot_general(
        first,
        second,
        (((first_dim,), (second_dim,)), ((), ())),
        preferred_element_type=jnp.float32,
    )


def product(first, second, first_dim, second_dim):
    first_high, first_low = halves(first)
    second_high, second_low = halves(second)
    small = one_pass(first_low, second_high, first_dim, second_dim) + one_pass(
        first_high, second_low, first_dim, second_dim
    )
    return small + one_pass(first_high, second_high, first_dim, second_dim)


@jax.custom_vjp
def mul_nn(first, second):
    return product(first, second, 1, 0)


@jax.custom_vjp
def mul_nt(first, second):
    return product(first, second, 1, 1)


@jax.custom_vjp
def mul_tn(first, second):
    return product(first, second, 0, 0)


mul_nn.defvjp(
    lambda a, b: (product(a, b, 1, 0), (a, b)),
    lambda res, ct: (product(ct, res[1], 1, 1), product(res[0], ct, 0, 0)),
)
mul_nt.defvjp(
    lambda a, b: (product(a, b, 1, 1), (a, b)),
    lambda res, ct: (product(ct, res[1], 1, 0), product(ct, res[0], 0, 0)),
)
mul_tn.defvjp(
    lambda a, b: (product(a, b, 0, 0), (a, b)),
    lambda res, ct: (product(res[1], ct, 1, 1), product(res[0], ct, 1, 0)),
)


@jax.custom_vjp
def solve_with(inverse, lower, rhs):
    return product(inverse, rhs, 1, 0)


def solve_forward(inverse, lower, rhs):
    solved = product(inverse, rhs, 1, 0)
    return solved, (inverse, solved)


def solve_backward(res, ct):
    inverse, solved = res
    rhs_grad = product(inverse, ct, 0, 0)
    return jnp.zeros_like(inverse), -product(rhs_grad, solved, 1, 1), rhs_grad


solve_with.defvjp(solve_forward, solve_backward)


def square_masks(size):
    rows = lax.broadcasted_iota(jnp.int32, (size, size), 0)
    cols = lax.broadcasted_iota(jnp.int32, (size, size), 1)
    return rows, cols


def unit_lower_inverse(lower):
    size = lower.shape[0]
    rows, cols = square_masks(size)
    inverse = jnp.where(rows == cols, 1.0, 0.0).astype(jnp.float32)
    level = 0
    while (1 << level) < size:
        width = 1 << level
        joined = (rows // (2 * width)) == (cols // (2 * width))
        mask = joined & ((rows // width) > (cols // width))
        off = jnp.where(mask, lower, 0.0)
        if level == 0:
            inverse = inverse - off
        else:
            inverse = inverse - product(product(inverse, off, 1, 0), inverse, 1, 0)
        level += 1
    return inverse


def silu_rows(x):
    return x * lax.logistic(x)


def unit_rows(matrix):
    return matrix * lax.rsqrt(jnp.sum(matrix * matrix, axis=1, keepdims=True) + epsilon)


def piece_terms(query_in, key_in, value_in, decay, strength, nn, nt):
    size = query_in.shape[0]
    width = query_in.shape[1]
    rows, cols = square_masks(size)
    strict = rows > cols
    inclusive = rows >= cols
    ones_low = jnp.where(inclusive, 1.0, 0.0).astype(jnp.float32)
    ones_high = jnp.where(rows < cols, 1.0, 0.0).astype(jnp.float32)
    queries = unit_rows(silu_rows(query_in)) * (1.0 / math.sqrt(width))
    keys = unit_rows(silu_rows(key_in))
    values = silu_rows(value_in)
    gaps = nn(ones_low, jnp.where(strict, jnp.broadcast_to(decay, (size, size)), 0.0))
    spread = jnp.exp(gaps)
    decay_wide = jnp.broadcast_to(decay, (size, width))
    head_decay = jnp.exp(nn(ones_low, decay_wide))
    tail_decay = jnp.exp(nn(ones_high, decay_wide))
    final = jnp.exp(jnp.sum(decay, axis=0, keepdims=True))
    lower = jnp.where(strict, spread * nt(keys, keys), 0.0) * strength
    scores = jnp.where(inclusive, spread * nt(queries, keys), 0.0)
    return (
        lower,
        scores,
        head_decay * queries,
        head_decay * keys,
        tail_decay * keys,
        values,
        final,
    )


def plain_nn(a, b):
    return product(a, b, 1, 0)


def plain_nt(a, b):
    return product(a, b, 1, 1)


def forward_kernel(q_ref, k_ref, v_ref, d_ref, s_ref, x_ref, o_ref, e_ref, m_ref, f_ref):
    strength = s_ref[...]
    lower, scores, led_queries, led_keys, tail_keys, values, final = piece_terms(
        q_ref[...], k_ref[...], v_ref[...], d_ref[...], strength, plain_nn, plain_nt
    )
    inverse = unit_lower_inverse(lower)
    x_ref[...] = inverse
    direct = product(inverse, strength * values, 1, 0)
    across = product(inverse, strength * led_keys, 1, 0)
    o_ref[...] = product(scores, direct, 1, 0)
    e_ref[...] = led_queries - product(scores, across, 1, 0)
    width = led_keys.shape[1]
    rows, cols = square_masks(width)
    m_ref[...] = jnp.where(rows == cols, jnp.broadcast_to(final, (width, width)), 0.0) - product(
        tail_keys, across, 0, 0
    )
    f_ref[...] = product(tail_keys, direct, 0, 0)


def backward_kernel(
    q_ref, k_ref, v_ref, d_ref, s_ref, x_ref, i_ref, g_ref, t_ref,
    dq_ref, dk_ref, dv_ref, dd_ref, ds_ref,
):
    inverse = x_ref[...]
    start = i_ref[...]

    def run(query_in, key_in, value_in, decay, strength):
        lower, scores, led_queries, led_keys, tail_keys, values, final = piece_terms(
            query_in, key_in, value_in, decay, strength, mul_nn, mul_nt
        )
        update = solve_with(inverse, lower, strength * (values - mul_nn(led_keys, start)))
        mixed = mul_nn(led_queries, start) + mul_nn(scores, update)
        last = final * start + mul_tn(tail_keys, update)
        return mixed, last

    unused, pull = jax.vjp(run, q_ref[...], k_ref[...], v_ref[...], d_ref[...], s_ref[...])
    grads = pull((g_ref[...], t_ref[...]))
    for ref, grad in zip((dq_ref, dk_ref, dv_ref, dd_ref, ds_ref), grads):
        ref[...] = grad


def out_gate(mixer_rows, gate_rows, gain_row):
    scale = lax.rsqrt(jnp.mean(mixer_rows * mixer_rows, axis=1, keepdims=True) + epsilon)
    return mixer_rows * scale * gain_row * silu_rows(gate_rows)


def gate_kernel(o_ref, e_ref, i_ref, gate_ref, gain_ref, out_ref):
    mixer_rows = o_ref[...] + product(e_ref[...], i_ref[...], 1, 0)
    gated = out_gate(mixer_rows, gate_ref[...].astype(jnp.float32), gain_ref[...])
    out_ref[...] = gated.astype(out_ref.dtype)


def gate_back_kernel(
    o_ref, e_ref, i_ref, gate_ref, gain_ref, grad_ref, mg_ref, gg_ref, ng_ref, r_ref
):
    effect = e_ref[...]
    mixer_rows = o_ref[...] + product(effect, i_ref[...], 1, 0)
    unused, pull = jax.vjp(
        out_gate, mixer_rows, gate_ref[...].astype(jnp.float32), gain_ref[...]
    )
    mixer_grad, gate_grad, gain_grad = pull(grad_ref[...].astype(jnp.float32))
    mg_ref[...] = mixer_grad
    gg_ref[...] = gate_grad.astype(gg_ref.dtype)
    ng_ref[...] = gain_grad
    r_ref[...] = product(effect, mixer_grad, 0, 0)


def per_head(kernel, grid, ins, outs, args, flops):
    return pl.pallas_call(
        kernel,
        grid=grid,
        in_specs=ins,
        out_specs=[spec for spec, _ in outs],
        out_shape=[shape for _, shape in outs],
        cost_estimate=pl.CostEstimate(
            flops=flops, bytes_accessed=sum(a.size * a.dtype.itemsize for a in args), transcendentals=0
        ),
    )(*args)


def columns(rows, width, first):
    return pl.BlockSpec((rows, width), lambda h, c, first=first: (c, first + h))


def heads_spec(*shape):
    return pl.BlockSpec((None, None) + shape, lambda h, c: (h, c) + (0,) * len(shape))


def of_shape(shape, kind=jnp.float32):
    return jax.ShapeDtypeStruct(shape, kind)


def state_product(state_map, held):
    return jnp.einsum("hij,hjv->hiv", state_map, held, precision=highest_precision)


def state_pull(state_map, held):
    return jnp.einsum("hji,hjv->hiv", state_map, held, precision=highest_precision)


def mat_nt(first_mat, second_mat):
    return lax.dot_general(
        first_mat, second_mat, (((1,), (1,)), ((), ())), preferred_element_type=jnp.float32
    )


def mat_tn(first_mat, second_mat):
    return lax.dot_general(
        first_mat, second_mat, (((0,), (0,)), ((), ())), preferred_element_type=jnp.float32
    )


def mat_nn(first_mat, second_mat):
    return jnp.dot(first_mat, second_mat, preferred_element_type=jnp.float32)


def rms_scale(hidden, gain_vec):
    return (
        hidden * lax.rsqrt(jnp.mean(hidden * hidden, axis=-1, keepdims=True) + epsilon) * gain_vec
    )


def swiglu(gate_part, up_part):
    return jax.nn.silu(gate_part) * up_part


def short_conv(padded, conv_all):
    length = padded.shape[0] - (KW - 1)
    mixed_rows = padded[0:length] * conv_all[0]
    for tap_index in range(1, KW):
        mixed_rows = mixed_rows + padded[tap_index : tap_index + length] * conv_all[tap_index]
    return mixed_rows


def decay_rates(rates, decay_log, decay_bias):
    heads = decay_log.shape[0]
    pairs = jnp.transpose(rates.reshape(rates.shape[0], heads, 2), (2, 1, 0))
    log_decay = -jnp.exp(decay_log)[:, None] * jax.nn.softplus(pairs[0] + decay_bias[:, None])
    strength = jax.nn.sigmoid(pairs[1])
    return log_decay[:, :, None], strength[:, :, None]


def split_columns(matrix, widths):
    pieces = []
    offset_col = 0
    for width_one in widths:
        pieces.append(matrix[:, offset_col : offset_col + width_one])
        offset_col = offset_col + width_one
    return pieces


def head_halves(weights, parts):
    slabs = []
    for part in range(parts):
        cut = []
        for weight in weights:
            width = weight.shape[1] // parts
            cut.append(weight[:, part * width : (part + 1) * width])
        slabs.append(jnp.concatenate(cut, axis=1))
    return jnp.stack(slabs)


def swap_halves(slabs):
    if slabs.shape[0] == 2:
        me = lax.axis_index("head")
        sent = lax.dynamic_index_in_dim(slabs, 1 - me, 0, keepdims=False)
        kept = lax.dynamic_index_in_dim(slabs, me, 0, keepdims=False)
        moved = lax.ppermute(sent, "head", [(0, 1), (1, 0)])
        return jnp.where(me == 0, jnp.stack([kept, moved]), jnp.stack([moved, kept]))
    return lax.all_to_all(slabs, "head", split_axis=0, concat_axis=0, tiled=True)


def whole_rows(slabs):
    full = lax.all_gather(slabs, ("ctx", "batch"), axis=1, tiled=True)
    return full.reshape(full.shape[0] * full.shape[1], full.shape[2])


def other_parts(block):
    parts = lax.axis_size("head")
    total = None
    for shift in range(1, parts):
        moved = lax.ppermute(block, "head", [(i, (i + shift) % parts) for i in range(parts)])
        moved = moved.astype(jnp.float32)
        total = moved if total is None else total + moved
    return total


def head_sum(partial, kind=jnp.bfloat16):
    sent = partial.astype(kind)
    if lax.axis_size("head") == 1:
        return sent.astype(jnp.float32)
    return sent.astype(jnp.float32) + other_parts(sent)


def own_rows_sum(partial):
    parts = lax.axis_size("head")
    rows = partial.shape[0] // parts
    me = lax.axis_index("head")
    total = lax.dynamic_slice_in_dim(partial, me * rows, rows, 0)
    for shift in range(1, parts):
        target = lax.rem(me + shift, parts)
        sent = lax.dynamic_slice_in_dim(partial, target * rows, rows, 0).astype(jnp.bfloat16)
        route = [(i, (i + shift) % parts) for i in range(parts)]
        total = total + lax.ppermute(sent, "head", route).astype(jnp.float32)
    return total


MESH_ID = pl.DeviceIdType.MESH
PAIR = 2


def staged(rows):
    parts = lax.axis_size("ctx") * lax.axis_size("batch")
    return lax.axis_size("batch") == 2 * PAIR and rows % parts == 0 and (rows // parts) % 16 == 0


def places():
    c = lax.axis_index("ctx")
    b = lax.axis_index("batch")
    k = lax.rem(b, PAIR)
    x = lax.div(b, PAIR)
    return c, x, k, x * PAIR + (1 - k), (1 - x) * PAIR + k


def greet(n, partner, across, c, facing=None):
    barrier = pltpu.get_barrier_semaphore()
    count = n + 1
    if facing is not None:
        pl.semaphore_signal(barrier, inc=1, device_id={"head": facing}, device_id_type=MESH_ID)
        count += 1
    for shift in range(1, n):
        pl.semaphore_signal(
            barrier, inc=1, device_id={"ctx": lax.rem(c + shift, n)}, device_id_type=MESH_ID
        )
    for other in (partner, across):
        pl.semaphore_signal(barrier, inc=1, device_id={"batch": other}, device_id_type=MESH_ID)
    pl.semaphore_wait(barrier, count)


def scatter_kernel(
    n, steps, widths, a_ref, sm_ref, *refs
):
    outs = refs[: len(widths)]
    (
        sm_out, from_pair, paired, from_across, held, from_left, from_right, acc,
        sm_in, sm_sent, sm_all,
        pair_send, pair_recv, cross_send, cross_recv, line_send, left_recv, right_recv,
        sm_send, sm_recv, all_send, all_recv,
    ) = refs[len(widths) :]
    c, x, k, partner, across = places()
    right = jnp.minimum(c + 1, n - 1)
    left = jnp.maximum(c - 1, 0)
    greet(n, partner, across, c)

    def to_pair(q):
        return pltpu.make_async_remote_copy(
            a_ref.at[:, :, 1 - k, q], from_pair.at[q], pair_send.at[q], pair_recv.at[q],
            device_id={"batch": partner}, device_id_type=MESH_ID,
        )

    def to_across(q):
        return pltpu.make_async_remote_copy(
            paired.at[q, 1 - x], from_across.at[q], cross_send.at[q], cross_recv.at[q],
            device_id={"batch": across}, device_id_type=MESH_ID,
        )

    def to_right(q, at):
        return pltpu.make_async_remote_copy(
            held.at[q, at], from_left.at[q, at], line_send.at[q, at], left_recv.at[q, at],
            device_id={"ctx": right}, device_id_type=MESH_ID,
        )

    def to_left(q, at):
        return pltpu.make_async_remote_copy(
            held.at[q, at], from_right.at[q, at], line_send.at[q, at], right_recv.at[q, at],
            device_id={"ctx": left}, device_id_type=MESH_ID,
        )

    def small(source, stage, other):
        return pltpu.make_async_remote_copy(
            source, sm_in.at[stage], sm_send.at[stage], sm_recv.at[stage],
            device_id={"batch": other}, device_id_type=MESH_ID,
        )

    def small_all(shift):
        peer = lax.rem(c + shift, n)
        return pltpu.make_async_remote_copy(
            sm_sent.at[1], sm_all.at[c], all_send.at[shift], all_recv.at[n - shift],
            device_id={"ctx": peer}, device_id_type=MESH_ID,
        )

    def small_from(shift):
        peer = lax.rem(c + shift, n)
        return pltpu.make_async_remote_copy(
            sm_sent.at[1], sm_all.at[peer], all_send.at[shift], all_recv.at[shift],
            device_id={"ctx": peer}, device_id_type=MESH_ID,
        )

    def begin(q, carry):
        to_pair(q).start()
        return carry

    lax.fori_loop(0, steps, begin, 0)
    first_small = small(sm_ref, 0, partner)
    first_small.start()

    def pair_up(q, carry):
        to_pair(q).wait_recv()

        def add(at, inner):
            for side in range(2):
                total = a_ref[at, side, k, q].astype(jnp.float32) + from_pair[
                    q, at, side
                ].astype(jnp.float32)
                paired[q, side, at] = total.astype(jnp.bfloat16)
            return inner

        lax.fori_loop(0, n, add, 0)
        to_across(q).start()
        return carry

    lax.fori_loop(0, steps, pair_up, 0)
    first_small.wait()
    sm_sent[0] = sm_ref[...] + sm_in[0]
    second_small = small(sm_sent.at[0], 1, across)
    second_small.start()

    def cross_up(q):
        to_across(q).wait_recv()

        def add(at, inner):
            total = paired[q, x, at].astype(jnp.float32) + from_across[q, at].astype(jnp.float32)
            held[q, at] = total.astype(jnp.bfloat16)
            return inner

        lax.fori_loop(0, n, add, 0)

        @pl.when(c == 0)
        def _():
            for at in range(n - 1, 0, -1):
                to_right(q, at).start()

        @pl.when(c == n - 1)
        def _():
            for at in range(n - 1):
                to_left(q, at).start()

    def relay(q):
        for near in range(n - 2):
            far = n - 1 - near

            @pl.when((c > 0) & (c < far))
            def _():
                to_right(q, far).wait_recv()
                total = held[q, far].astype(jnp.float32) + from_left[q, far].astype(jnp.float32)
                held[q, far] = total.astype(jnp.bfloat16)
                to_right(q, far).start()

            @pl.when((c < n - 1) & (c > near))
            def _():
                to_left(q, near).wait_recv()
                total = held[q, near].astype(jnp.float32) + from_right[q, near].astype(
                    jnp.float32
                )
                held[q, near] = total.astype(jnp.bfloat16)
                to_left(q, near).start()

        acc[...] = paired[q, x, c].astype(jnp.float32) + from_across[q, c].astype(jnp.float32)

        @pl.when(c > 0)
        def _():
            to_right(q, c).wait_recv()
            acc[...] += from_left[q, c].astype(jnp.float32)

        @pl.when(c < n - 1)
        def _():
            to_left(q, c).wait_recv()
            acc[...] += from_right[q, c].astype(jnp.float32)

        first = 0
        for out, width in zip(outs, widths):
            out[q] = acc[:, first : first + width]
            first += width

    cross_up(0)
    second_small.wait()
    sm_sent[1] = sm_sent[0] + sm_in[1]
    for shift in range(1, n):
        small_all(shift).start()

    def middle(q, carry):
        cross_up(q + 1)
        relay(q)
        return carry

    lax.fori_loop(0, steps - 1, middle, 0)
    relay(steps - 1)
    sm_all[c] = sm_sent[1]
    for shift in range(1, n):
        small_from(shift).wait_recv()
        small_all(shift).wait_send()
    total = sm_all[0]
    for at in range(1, n):
        total = total + sm_all[at]
    sm_out[...] = total

    def drain(q, carry):
        to_pair(q).wait_send()
        to_across(q).wait_send()

        def line(at, inner):
            @pl.when(at > c)
            def _():
                to_right(q, at).wait_send()

            @pl.when(at < c)
            def _():
                to_left(q, at).wait_send()

            return inner

        lax.fori_loop(0, n, line, 0)
        return carry

    lax.fori_loop(0, steps, drain, 0)


def scatter_sum(products, smalls, widths):
    n = lax.axis_size("ctx")
    parts = n * lax.axis_size("batch")
    rows = products.shape[0] // parts
    cols = products.shape[1]
    steps = rows // 16
    blocks = products.reshape(n, 2, 2, steps, 16, cols)
    count = smalls.shape[0]
    lanes = pl.cdiv(count, 1024) * 8
    flat = jnp.pad(smalls, (0, lanes * 128 - count)).reshape(lanes, 128)
    vmem = pl.BlockSpec(memory_space=pltpu.VMEM)
    half = jnp.bfloat16
    dma = pltpu.SemaphoreType.DMA
    results = pl.pallas_call(
        functools.partial(scatter_kernel, n, steps, widths),
        in_specs=[vmem, vmem],
        out_specs=[vmem] * (len(widths) + 1),
        out_shape=[of_shape((steps, 16, width)) for width in widths] + [of_shape(flat.shape)],
        scratch_shapes=[
            pltpu.VMEM((steps, n, 2, 16, cols), half),
            pltpu.VMEM((steps, 2, n, 16, cols), half),
            pltpu.VMEM((steps, n, 16, cols), half),
            pltpu.VMEM((steps, n, 16, cols), half),
            pltpu.VMEM((steps, n, 16, cols), half),
            pltpu.VMEM((steps, n, 16, cols), half),
            pltpu.VMEM((16, cols), jnp.float32),
            pltpu.VMEM((2,) + flat.shape, jnp.float32),
            pltpu.VMEM((2,) + flat.shape, jnp.float32),
            pltpu.VMEM((n,) + flat.shape, jnp.float32),
            dma((steps,)), dma((steps,)), dma((steps,)), dma((steps,)),
            dma((steps, n)), dma((steps, n)), dma((steps, n)),
            dma((2,)), dma((2,)), dma((n,)), dma((n,)),
        ],
        compiler_params=pltpu.CompilerParams(collective_id=0, has_side_effects=True),
        cost_estimate=pl.CostEstimate(
            flops=0, bytes_accessed=4 * products.size * 2, transcendentals=0
        ),
    )(blocks, flat)
    sums = [result.reshape(rows, width) for result, width in zip(results, widths)]
    return sums, results[-1].reshape(-1)[:count]


def gather_kernel(n, slab_ref, tok_ref, cot_ref, *refs):
    (
        out, tok_out, cot_out,
        own_sem, side_send, side_recv, line_send, line_recv,
        cross_send, cross_recv, pair_send, pair_recv,
    ) = refs
    c, x, k, partner, across = places()
    me = lax.axis_index("head")
    other = 1 - me
    right = jnp.minimum(c + 1, n - 1)
    left = jnp.maximum(c - 1, 0)
    greet(n, partner, across, c, other)

    def copy(source, target, send, recv, axis, to):
        return pltpu.make_async_remote_copy(
            source, target, send, recv, device_id={axis: to}, device_id_type=MESH_ID
        )

    def piece(j, at, side, core):
        return out.at[me if j == 0 else other, at, side, core]

    def to_line(j, at, to, source=None):
        spot = piece(j, at, x, k)
        return copy(
            spot if source is None else source, spot,
            line_send.at[j, at], line_recv.at[j, at], "ctx", to,
        )

    def to_across(j, at, side, source=None):
        spot = piece(j, at, side, k)
        return copy(
            spot if source is None else source, spot,
            cross_send.at[j, at], cross_recv.at[j, at], "batch", across,
        )

    def to_pair(j, at, side, core, source=None):
        spot = piece(j, at, side, core)
        return copy(
            spot if source is None else source, spot,
            pair_send.at[j, at, side], pair_recv.at[j, at, side], "batch", partner,
        )

    swap = copy(
        slab_ref.at[other], out.at[me, c, x, k], side_send.at[0], side_recv.at[0], "head", other
    )
    tok_swap = copy(tok_ref, tok_out.at[me], side_send.at[1], side_recv.at[1], "head", other)
    cot_swap = copy(cot_ref, cot_out.at[me], side_send.at[2], side_recv.at[2], "head", other)
    swap.start()

    def own(j, source):
        to_across(j, c, x, source).start()

        @pl.when(c < n - 1)
        def _():
            copy(
                source, piece(j, c, x, k), own_sem.at[3 + j], line_recv.at[j, c], "ctx", right
            ).start()

        @pl.when(c > 0)
        def _():
            copy(
                source, piece(j, c, x, k), own_sem.at[5 + j], line_recv.at[j, c], "ctx", left
            ).start()

        to_pair(j, c, x, k, source).start()

    kept = slab_ref.at[me]
    own(0, kept)
    locals_ = (
        pltpu.make_async_copy(kept, out.at[me, c, x, k], own_sem.at[0]),
        pltpu.make_async_copy(tok_ref, tok_out.at[me], own_sem.at[1]),
        pltpu.make_async_copy(cot_ref, cot_out.at[me], own_sem.at[2]),
    )
    for one in locals_:
        one.start()
    from_side = copy(
        slab_ref.at[other], out.at[other, c, x, k], side_send.at[0], side_recv.at[0], "head", other
    )
    from_side.wait_recv()
    own(1, piece(1, c, x, k))
    tok_swap.start()
    cot_swap.start()

    def cross_done(j, at):
        to_across(j, at, 1 - x).wait_recv()
        to_pair(j, at, 1 - x, k).start()

    for distance in range(1, n + 1):
        for j in range(2):
            for sign in (-1, 1):
                at = c + sign * distance
                back = c + sign * (distance - 1)
                onward = right if sign < 0 else left
                more = (c < n - 1) if sign < 0 else (c > 0)
                if distance < n:

                    @pl.when((at >= 0) & (at < n))
                    def _():
                        to_line(j, at, onward).wait_recv()

                        @pl.when(more)
                        def _():
                            to_line(j, at, onward).start()

                        to_across(j, at, x).start()
                        to_pair(j, at, x, k).start()

                if distance > 1:

                    @pl.when((back >= 0) & (back < n))
                    def _():
                        cross_done(j, back)

                elif sign < 0:
                    cross_done(j, c)

    for j in range(2):

        def settle(at, carry):
            for side in range(2):
                to_pair(j, at, side, 1 - k).wait_recv()
                to_pair(j, at, side, k).wait_send()
            to_across(j, at, x).wait_send()

            @pl.when(((at < c) & (c < n - 1)) | ((at > c) & (c > 0)))
            def _():
                to_line(j, at, right).wait_send()

            return carry

        lax.fori_loop(0, n, settle, 0)
        spot = piece(j, c, x, k)

        @pl.when(c < n - 1)
        def _():
            copy(spot, spot, own_sem.at[3 + j], line_recv.at[j, c], "ctx", right).wait_send()

        @pl.when(c > 0)
        def _():
            copy(spot, spot, own_sem.at[5 + j], line_recv.at[j, c], "ctx", left).wait_send()

    for one in locals_:
        one.wait()
    swap.wait_send()
    for sent, target, slot in ((tok_swap, tok_out, 1), (cot_swap, cot_out, 2)):
        sent.wait_send()
        copy(
            target.at[other], target.at[other], side_send.at[slot], side_recv.at[slot], "head", other
        ).wait_recv()


def gathers(slabs):
    return (
        lax.axis_size("head") == 2
        and lax.axis_size("batch") == 2 * PAIR
        and slabs.shape[1] % 16 == 0
    )


def gather_all(slabs, tok, cot):
    n = lax.axis_size("ctx")
    rows, cols = slabs.shape[1:]
    vmem = pl.BlockSpec(memory_space=pltpu.VMEM)
    anywhere = pl.BlockSpec(memory_space=pl.ANY)
    dma = pltpu.SemaphoreType.DMA
    half = jnp.bfloat16
    weight, tokens, cots = pl.pallas_call(
        functools.partial(gather_kernel, n),
        in_specs=[vmem] * 3,
        out_specs=[anywhere] * 3,
        out_shape=[
            of_shape((2, n, 2, 2, rows, cols), half),
            of_shape((2,) + tok.shape, half),
            of_shape((2,) + cot.shape, half),
        ],
        scratch_shapes=[
            dma((7,)), dma((3,)), dma((3,)), dma((2, n)), dma((2, n)),
            dma((2, n)), dma((2, n)), dma((2, n, 2)), dma((2, n, 2)),
        ],
        compiler_params=pltpu.CompilerParams(collective_id=1, has_side_effects=True),
        cost_estimate=pl.CostEstimate(
            flops=0, bytes_accessed=64 * n * rows * cols, transcendentals=0
        ),
    )(slabs, tok, cot)
    return (
        weight.reshape(8 * n * rows, cols),
        tokens.reshape(-1, tok.shape[1]),
        cots.reshape(-1, cot.shape[1]),
    )


def outer_kernel(*refs):
    out = refs[-1]
    first = 0
    for left_ref, right_ref in zip(refs[:-1:2], refs[1:-1:2]):
        width = right_ref.shape[1]
        part = one_pass(left_ref[...], right_ref[...], 0, 0)
        out[:, first : first + width] = part.astype(out.dtype)
        first += width


def outer_products(*pairs):
    tokens, features = pairs[0][0].shape
    block = min(256, features)
    total = sum(second.shape[1] for _, second in pairs)
    specs = []
    for _, second in pairs:
        specs.append(pl.BlockSpec((tokens, block), lambda i: (0, i)))
        specs.append(pl.BlockSpec(second.shape, lambda i: (0, 0)))
    args = [one for pair in pairs for one in pair]
    return pl.pallas_call(
        outer_kernel,
        grid=(features // block,),
        in_specs=specs,
        out_specs=pl.BlockSpec((block, total), lambda i: (i, 0)),
        out_shape=of_shape((features, total), jnp.bfloat16),
        cost_estimate=pl.CostEstimate(
            flops=2 * tokens * features * total,
            bytes_accessed=2 * features * total,
            transcendentals=0,
        ),
    )(*args)


def body(
    tokens,
    cotangent,
    norm1_gain,
    w_query,
    w_key,
    w_value,
    w_gate,
    w_rates,
    conv_query,
    conv_key,
    conv_value,
    decay_log,
    decay_bias,
    out_gain,
    w_out,
    norm2_gain,
    w_ffgate,
    w_ffup,
    w_down,
):
    parts = lax.axis_size("head")
    me = lax.axis_index("head")
    heads = decay_log.shape[0]
    query_width = conv_query.shape[1]
    value_width = conv_value.shape[1]
    dk = query_width // heads
    dv = value_width // heads
    margin = KW - 1
    gains = jnp.stack([norm1_gain, norm2_gain], axis=1)
    slabs_in = head_halves(
        [w_query, w_key, w_value, w_gate, w_rates, jnp.tile(gains, (1, parts))], parts
    )
    rates_width = w_rates.shape[1] // parts
    mixed_width = 2 * query_width + value_width
    proj_width = mixed_width + value_width + rates_width
    later = swap_halves(head_halves([w_out, w_ffgate, w_ffup, w_down], parts))
    ff_local = w_down.shape[1] // parts
    if gathers(slabs_in):
        later, slabs_in = lax.optimization_barrier((later, slabs_in))
        later_weight = whole_rows(later)
        in_weight, piece_tok, cot = gather_all(slabs_in, tokens[0], cotangent[0])
    else:
        in_weight = whole_rows(swap_halves(slabs_in))
        later_weight = whole_rows(later)
        piece_tok = lax.all_gather(tokens[0], "head", axis=0, tiled=True)
        cot = lax.all_gather(cotangent[0], "head", axis=0, tiled=True)
    gain_cols = in_weight[:, proj_width:].astype(jnp.float32)
    gain_one = gain_cols[:, 0]
    gain_two = gain_cols[:, 1]
    out_weight = later_weight[:, :value_width]
    ff_weight = later_weight[:, value_width : value_width + 2 * ff_local]
    down_weight = later_weight[:, value_width + 2 * ff_local :]

    inputs_tok = tokens[0]
    own_count = inputs_tok.shape[0]
    residual = piece_tok.astype(jnp.float32)
    piece_rows = residual.shape[0]
    normed_one = rms_scale(residual, gain_one).astype(jnp.bfloat16)
    proj = mat_nn(normed_one, in_weight[:, :proj_width]).astype(jnp.bfloat16)
    joined = proj[:, :mixed_width]
    rates_here = proj[:, mixed_width + value_width :]
    rim_rows = passed_along(joined[piece_rows - margin :], "ctx", 1)
    padded = jnp.concatenate([rim_rows, joined], axis=0).astype(jnp.float32)
    conv_all = jnp.concatenate([conv_query, conv_key, conv_value], axis=1).astype(jnp.float32)
    mixed, conv_vjp = jax.vjp(short_conv, padded, conv_all)
    (log_decay, strength), rates_vjp = jax.vjp(
        decay_rates, rates_here.astype(jnp.float32), decay_log, decay_bias
    )
    value_first = 2 * query_width // dv
    chunk = min(CHUNK, piece_rows)
    chunks = piece_rows // chunk
    grid = (heads, chunks)
    log_decay = log_decay.reshape(heads, chunks, chunk, 1)
    strength = strength.reshape(heads, chunks, chunk, 1)
    mixed_specs = [
        columns(chunk, dk, 0),
        columns(chunk, dk, heads),
        columns(chunk, dv, value_first),
        heads_spec(chunk, 1),
        heads_spec(chunk, 1),
    ]
    square = heads_spec(chunk, chunk)
    state = heads_spec(dk, dv)
    rows_v = columns(chunk, dv, 0)
    rows_k = columns(chunk, dk, 0)
    inverse, local_out, effect, state_map, state_offset = per_head(
        forward_kernel,
        grid,
        mixed_specs,
        [
            (square, of_shape((heads, chunks, chunk, chunk))),
            (rows_v, of_shape((piece_rows, value_width))),
            (rows_k, of_shape((piece_rows, query_width))),
            (heads_spec(dk, dk), of_shape((heads, chunks, dk, dk))),
            (state, of_shape((heads, chunks, dk, dv))),
        ],
        (mixed, mixed, mixed, log_decay, strength),
        heads * 100 * piece_rows * chunk**2,
    )
    chunk_maps = [state_map[:, i] for i in range(chunks)]
    chunk_offsets = [state_offset[:, i] for i in range(chunks)]
    piece_map = chunk_maps[0]
    piece_offset = chunk_offsets[0]
    for i in range(1, chunks):
        piece_map = state_product(chunk_maps[i], piece_map)
        piece_offset = state_product(chunk_maps[i], piece_offset) + chunk_offsets[i]
    last_step = lax.axis_size("ctx") - 1
    start_state = jnp.zeros_like(piece_offset)
    for step in range(last_step):
        moved = piece_offset
        if step > 0:
            moved = moved + state_product(piece_map, start_state)
        start_state = passed_along(moved.astype(jnp.bfloat16), "ctx", 1).astype(jnp.float32)
    starts = [start_state]
    for i in range(1, chunks):
        starts.append(state_product(chunk_maps[i - 1], starts[-1]) + chunk_offsets[i - 1])
    start_states = jnp.stack(starts, axis=1)
    gain_row = out_gain.astype(jnp.float32)[None]
    gate_spec = columns(chunk, dv, mixed_width // dv)
    gain_spec = pl.BlockSpec((1, dv), lambda h, c: (0, h))
    gain_out = pl.BlockSpec((None, 1, dv), lambda h, c: (c, 0, h))
    gate_ins = [rows_v, rows_k, state, gate_spec, gain_spec]
    gate_args = (local_out, effect, start_states, proj, gain_row)
    (gated,) = per_head(
        gate_kernel,
        grid,
        gate_ins,
        [(rows_v, of_shape((piece_rows, value_width), jnp.bfloat16))],
        gate_args,
        heads * 12 * piece_rows * dk * dv,
    )
    middle = residual + head_sum(mat_nt(gated, out_weight))
    normed_two_f, norm_two_vjp = jax.vjp(rms_scale, middle, gain_two)
    normed_two = normed_two_f.astype(jnp.bfloat16)
    ff_both = mat_nn(normed_two, ff_weight)
    hidden_f, swiglu_vjp = jax.vjp(swiglu, ff_both[:, :ff_local], ff_both[:, ff_local:])
    hidden = hidden_f.astype(jnp.bfloat16)
    hidden_grad = mat_nn(cot, down_weight)
    gate_grad_f, up_grad_f = swiglu_vjp(hidden_grad)
    ff_grads = jnp.concatenate([gate_grad_f, up_grad_f], axis=1).astype(jnp.bfloat16)
    middle_part, gain_two_grad = norm_two_vjp(head_sum(mat_nt(ff_grads, ff_weight)))
    middle_grad = cot.astype(jnp.float32) + middle_part
    middle_grad_b = middle_grad.astype(jnp.bfloat16)
    gated_grad = mat_nn(middle_grad_b, out_weight).astype(jnp.bfloat16)
    middle_own = lax.dynamic_slice_in_dim(middle, me * own_count, own_count, 0)
    output_tok = (middle_own + own_rows_sum(mat_nt(hidden, down_weight))).astype(jnp.bfloat16)

    mixer_grad, gate_bf, out_gain_grad, reach = per_head(
        gate_back_kernel,
        grid,
        gate_ins + [rows_v],
        [
            (rows_v, of_shape((piece_rows, value_width))),
            (rows_v, of_shape((piece_rows, value_width), jnp.bfloat16)),
            (gain_out, of_shape((chunks, 1, value_width))),
            (state, of_shape((heads, chunks, dk, dv))),
        ],
        gate_args + (gated_grad,),
        heads * 24 * piece_rows * dk * dv,
    )
    chunk_reach = [reach[:, i] for i in range(chunks)]
    piece_reach = chunk_reach[chunks - 1]
    for i in range(chunks - 2, -1, -1):
        piece_reach = chunk_reach[i] + state_pull(chunk_maps[i], piece_reach)
    last_grad = jnp.zeros_like(piece_reach)
    for step in range(last_step):
        moved = piece_reach
        if step > 0:
            moved = moved + state_pull(piece_map, last_grad)
        last_grad = passed_along(moved.astype(jnp.bfloat16), "ctx", -1).astype(jnp.float32)
    lasts = [last_grad]
    for i in range(chunks - 1, 0, -1):
        lasts.insert(0, chunk_reach[i] + state_pull(chunk_maps[i], lasts[0]))
    last_grads = jnp.stack(lasts, axis=1)

    ff_products = outer_products(
        (middle_grad_b, gated), (normed_two, ff_grads), (cot, hidden)
    )
    ff_sums = lax.psum_scatter(
        ff_products,
        ("ctx", "batch"),
        scatter_dimension=0,
        tiled=True,
    )

    query_g, key_g, value_g, decay_g, strength_g = per_head(
        backward_kernel,
        grid,
        mixed_specs + [square, state, rows_v, state],
        [
            (rows_k, of_shape((piece_rows, query_width))),
            (rows_k, of_shape((piece_rows, query_width))),
            (rows_v, of_shape((piece_rows, value_width))),
            (heads_spec(chunk, 1), of_shape((heads, chunks, chunk, 1))),
            (heads_spec(chunk, 1), of_shape((heads, chunks, chunk, 1))),
        ],
        (mixed, mixed, mixed, log_decay, strength, inverse, start_states, mixer_grad, last_grads),
        heads * 100 * piece_rows * chunk**2,
    )
    padded_grad, conv_grad = conv_vjp(jnp.concatenate([query_g, key_g, value_g], axis=1))
    rates_grad_f, decay_log_grad, decay_bias_grad = rates_vjp(
        (decay_g.reshape(heads, piece_rows, 1), strength_g.reshape(heads, piece_rows, 1))
    )
    back_rim = passed_along(padded_grad[:margin], "ctx", -1)
    own_rows = padded_grad[margin:]
    own_rows = jnp.concatenate(
        [own_rows[: piece_rows - margin], own_rows[piece_rows - margin :] + back_rim], axis=0
    ).astype(jnp.bfloat16)
    proj_grad = jnp.concatenate([own_rows, gate_bf, rates_grad_f.astype(jnp.bfloat16)], axis=1)
    proj_products = outer_products((normed_one, proj_grad))
    own_grad = own_rows_sum(mat_nt(proj_grad, in_weight[:, :proj_width]))
    unused_rows, norm_one_vjp = jax.vjp(rms_scale, inputs_tok.astype(jnp.float32), gain_one)
    input_part, gain_one_grad = norm_one_vjp(own_grad)
    input_grad = lax.dynamic_slice_in_dim(middle_grad, me * own_count, own_count, 0) + input_part
    smalls = (
        conv_grad.reshape(-1),
        jnp.sum(out_gain_grad, axis=(0, 1)),
        head_sum(gain_one_grad, jnp.float32),
        gain_two_grad,
        decay_log_grad,
        decay_bias_grad,
    )
    proj_widths = (query_width, query_width, value_width, value_width, rates_width)
    if staged(proj_products.shape[0]):
        proj_parts, summed = scatter_sum(proj_products, jnp.concatenate(smalls), proj_widths)
    else:
        proj_sums = lax.psum_scatter(
            proj_products, ("ctx", "batch"), scatter_dimension=0, tiled=True
        ).astype(jnp.float32)
        proj_parts = split_columns(proj_sums, proj_widths)
        summed = lax.psum(jnp.concatenate(smalls), ("ctx", "batch"))
    ff_parts = split_columns(
        ff_sums.astype(jnp.float32), (value_width, ff_local, ff_local, ff_local)
    )
    cuts = []
    first = 0
    for small in smalls:
        cuts.append(summed[first : first + small.shape[0]])
        first += small.shape[0]
    conv_sum = cuts[0].reshape(conv_grad.shape)
    share = norm1_gain.shape[0]
    place = (me * lax.axis_size("ctx") + lax.axis_index("ctx")) * lax.axis_size("batch")
    place = (place + lax.axis_index("batch")) * share
    return (
        output_tok[None],
        input_grad[None],
        lax.dynamic_slice_in_dim(cuts[2], place, share, 0),
        proj_parts[0],
        proj_parts[1],
        proj_parts[2],
        proj_parts[3],
        proj_parts[4],
        conv_sum[:, :query_width],
        conv_sum[:, query_width : 2 * query_width],
        conv_sum[:, 2 * query_width :],
        cuts[4],
        cuts[5],
        cuts[1],
        ff_parts[0],
        lax.dynamic_slice_in_dim(cuts[3], place, share, 0),
        ff_parts[1],
        ff_parts[2],
        ff_parts[3],
    )


def solution(mesh):
    placed = (
        P("batch", ("ctx", "head"), None),
        P("batch", ("ctx", "head"), None),
        P(("head", "ctx", "batch")),
        P(("head", "ctx", "batch"), None),
        P(("head", "ctx", "batch"), None),
        P(("head", "ctx", "batch"), None),
        P(("head", "ctx", "batch"), None),
        P(("head", "ctx", "batch"), None),
        P(None, "head"),
        P(None, "head"),
        P(None, "head"),
        P("head"),
        P("head"),
        P("head"),
        P(("head", "ctx", "batch"), None),
        P(("head", "ctx", "batch")),
        P(("head", "ctx", "batch"), None),
        P(("head", "ctx", "batch"), None),
        P(("head", "ctx", "batch"), None),
    )
    return jax.shard_map(
        body,
        mesh=mesh,
        in_specs=placed,
        out_specs=(
            P("batch", ("ctx", "head"), None),
            P("batch", ("ctx", "head"), None),
            P(("head", "ctx", "batch")),
            P(("ctx", "batch"), "head"),
            P(("ctx", "batch"), "head"),
            P(("ctx", "batch"), "head"),
            P(("ctx", "batch"), "head"),
            P(("ctx", "batch"), "head"),
            P(None, "head"),
            P(None, "head"),
            P(None, "head"),
            P("head"),
            P("head"),
            P("head"),
            P(("ctx", "batch"), "head"),
            P(("head", "ctx", "batch")),
            P(("ctx", "batch"), "head"),
            P(("ctx", "batch"), "head"),
            P(("ctx", "batch"), "head"),
        ),
        check_vma=False,
    )
```

```python
import functools
import math

import jax
import jax.numpy as jnp
from jax import lax
from jax.experimental import pallas as pl
from jax.experimental.pallas import tpu as pltpu
from jax.sharding import PartitionSpec as P

KW = 4
CHUNK = 256
epsilon = 1e-06
highest_precision = lax.Precision.HIGHEST


def passed_along(block, axis, distance):
    devices = range(lax.axis_size(axis))
    route = [(i - distance, i) for i in devices if i - distance in devices]
    return lax.ppermute(block, axis, route)


def halves(matrix):
    high = matrix.astype(jnp.bfloat16)
    return high, (matrix - high.astype(jnp.float32)).astype(jnp.bfloat16)


def one_pass(first, second, first_dim, second_dim):
    return lax.dot_general(
        first,
        second,
        (((first_dim,), (second_dim,)), ((), ())),
        preferred_element_type=jnp.float32,
    )


def product(first, second, first_dim, second_dim):
    first_high, first_low = halves(first)
    second_high, second_low = halves(second)
    small = one_pass(first_low, second_high, first_dim, second_dim) + one_pass(
        first_high, second_low, first_dim, second_dim
    )
    return small + one_pass(first_high, second_high, first_dim, second_dim)


@jax.custom_vjp
def mul_nn(first, second):
    return product(first, second, 1, 0)


@jax.custom_vjp
def mul_nt(first, second):
    return product(first, second, 1, 1)


@jax.custom_vjp
def mul_tn(first, second):
    return product(first, second, 0, 0)


mul_nn.defvjp(
    lambda a, b: (product(a, b, 1, 0), (a, b)),
    lambda res, ct: (product(ct, res[1], 1, 1), product(res[0], ct, 0, 0)),
)
mul_nt.defvjp(
    lambda a, b: (product(a, b, 1, 1), (a, b)),
    lambda res, ct: (product(ct, res[1], 1, 0), product(ct, res[0], 0, 0)),
)
mul_tn.defvjp(
    lambda a, b: (product(a, b, 0, 0), (a, b)),
    lambda res, ct: (product(res[1], ct, 1, 1), product(res[0], ct, 1, 0)),
)


@jax.custom_vjp
def solve_with(inverse, lower, rhs):
    return product(inverse, rhs, 1, 0)


def solve_forward(inverse, lower, rhs):
    solved = product(inverse, rhs, 1, 0)
    return solved, (inverse, solved)


def solve_backward(res, ct):
    inverse, solved = res
    rhs_grad = product(inverse, ct, 0, 0)
    return jnp.zeros_like(inverse), -product(rhs_grad, solved, 1, 1), rhs_grad


solve_with.defvjp(solve_forward, solve_backward)


def square_masks(size):
    rows = lax.broadcasted_iota(jnp.int32, (size, size), 0)
    cols = lax.broadcasted_iota(jnp.int32, (size, size), 1)
    return rows, cols


def unit_lower_inverse(lower):
    size = lower.shape[0]
    rows, cols = square_masks(size)
    inverse = jnp.where(rows == cols, 1.0, 0.0).astype(jnp.float32)
    level = 0
    while (1 << level) < size:
        width = 1 << level
        joined = (rows // (2 * width)) == (cols // (2 * width))
        mask = joined & ((rows // width) > (cols // width))
        off = jnp.where(mask, lower, 0.0)
        if level == 0:
            inverse = inverse - off
        else:
            inverse = inverse - product(product(inverse, off, 1, 0), inverse, 1, 0)
        level += 1
    return inverse


def silu_rows(x):
    return x * lax.logistic(x)


def unit_rows(matrix):
    return matrix * lax.rsqrt(jnp.sum(matrix * matrix, axis=1, keepdims=True) + epsilon)


def piece_terms(query_in, key_in, value_in, decay, strength, nn, nt):
    size = query_in.shape[0]
    width = query_in.shape[1]
    rows, cols = square_masks(size)
    strict = rows > cols
    inclusive = rows >= cols
    ones_low = jnp.where(inclusive, 1.0, 0.0).astype(jnp.float32)
    ones_high = jnp.where(rows < cols, 1.0, 0.0).astype(jnp.float32)
    queries = unit_rows(silu_rows(query_in)) * (1.0 / math.sqrt(width))
    keys = unit_rows(silu_rows(key_in))
    values = silu_rows(value_in)
    gaps = nn(ones_low, jnp.where(strict, jnp.broadcast_to(decay, (size, size)), 0.0))
    spread = jnp.exp(gaps)
    decay_wide = jnp.broadcast_to(decay, (size, width))
    head_decay = jnp.exp(nn(ones_low, decay_wide))
    tail_decay = jnp.exp(nn(ones_high, decay_wide))
    final = jnp.exp(jnp.sum(decay, axis=0, keepdims=True))
    lower = jnp.where(strict, spread * nt(keys, keys), 0.0) * strength
    scores = jnp.where(inclusive, spread * nt(queries, keys), 0.0)
    return (
        lower,
        scores,
        head_decay * queries,
        head_decay * keys,
        tail_decay * keys,
        values,
        final,
    )


def plain_nn(a, b):
    return product(a, b, 1, 0)


def plain_nt(a, b):
    return product(a, b, 1, 1)


def forward_kernel(q_ref, k_ref, v_ref, d_ref, s_ref, x_ref, o_ref, e_ref, m_ref, f_ref):
    strength = s_ref[...]
    lower, scores, led_queries, led_keys, tail_keys, values, final = piece_terms(
        q_ref[...], k_ref[...], v_ref[...], d_ref[...], strength, plain_nn, plain_nt
    )
    inverse = unit_lower_inverse(lower)
    x_ref[...] = inverse
    direct = product(inverse, strength * values, 1, 0)
    across = product(inverse, strength * led_keys, 1, 0)
    o_ref[...] = product(scores, direct, 1, 0)
    e_ref[...] = led_queries - product(scores, across, 1, 0)
    width = led_keys.shape[1]
    rows, cols = square_masks(width)
    m_ref[...] = jnp.where(rows == cols, jnp.broadcast_to(final, (width, width)), 0.0) - product(
        tail_keys, across, 0, 0
    )
    f_ref[...] = product(tail_keys, direct, 0, 0)


def backward_kernel(
    q_ref, k_ref, v_ref, d_ref, s_ref, x_ref, i_ref, g_ref, t_ref,
    dq_ref, dk_ref, dv_ref, dd_ref, ds_ref,
):
    inverse = x_ref[...]
    start = i_ref[...]

    def run(query_in, key_in, value_in, decay, strength):
        lower, scores, led_queries, led_keys, tail_keys, values, final = piece_terms(
            query_in, key_in, value_in, decay, strength, mul_nn, mul_nt
        )
        update = solve_with(inverse, lower, strength * (values - mul_nn(led_keys, start)))
        mixed = mul_nn(led_queries, start) + mul_nn(scores, update)
        last = final * start + mul_tn(tail_keys, update)
        return mixed, last

    unused, pull = jax.vjp(run, q_ref[...], k_ref[...], v_ref[...], d_ref[...], s_ref[...])
    grads = pull((g_ref[...], t_ref[...]))
    for ref, grad in zip((dq_ref, dk_ref, dv_ref, dd_ref, ds_ref), grads):
        ref[...] = grad


def out_gate(mixer_rows, gate_rows, gain_row):
    scale = lax.rsqrt(jnp.mean(mixer_rows * mixer_rows, axis=1, keepdims=True) + epsilon)
    return mixer_rows * scale * gain_row * silu_rows(gate_rows)


def gate_kernel(o_ref, e_ref, i_ref, gate_ref, gain_ref, out_ref):
    mixer_rows = o_ref[...] + product(e_ref[...], i_ref[...], 1, 0)
    gated = out_gate(mixer_rows, gate_ref[...].astype(jnp.float32), gain_ref[...])
    out_ref[...] = gated.astype(out_ref.dtype)


def gate_back_kernel(
    o_ref, e_ref, i_ref, gate_ref, gain_ref, grad_ref, mg_ref, gg_ref, ng_ref, r_ref
):
    effect = e_ref[...]
    mixer_rows = o_ref[...] + product(effect, i_ref[...], 1, 0)
    unused, pull = jax.vjp(
        out_gate, mixer_rows, gate_ref[...].astype(jnp.float32), gain_ref[...]
    )
    mixer_grad, gate_grad, gain_grad = pull(grad_ref[...].astype(jnp.float32))
    mg_ref[...] = mixer_grad
    gg_ref[...] = gate_grad.astype(gg_ref.dtype)
    ng_ref[...] = gain_grad
    r_ref[...] = product(effect, mixer_grad, 0, 0)


def per_head(kernel, grid, ins, outs, args, flops):
    return pl.pallas_call(
        kernel,
        grid=grid,
        in_specs=ins,
        out_specs=[spec for spec, _ in outs],
        out_shape=[shape for _, shape in outs],
        cost_estimate=pl.CostEstimate(
            flops=flops, bytes_accessed=sum(a.size * a.dtype.itemsize for a in args), transcendentals=0
        ),
    )(*args)


def columns(rows, width, first):
    return pl.BlockSpec((rows, width), lambda h, c, first=first: (c, first + h))


def heads_spec(*shape):
    return pl.BlockSpec((None, None) + shape, lambda h, c: (h, c) + (0,) * len(shape))


def of_shape(shape, kind=jnp.float32):
    return jax.ShapeDtypeStruct(shape, kind)


def state_product(state_map, held):
    return jnp.einsum("hij,hjv->hiv", state_map, held, precision=highest_precision)


def state_pull(state_map, held):
    return jnp.einsum("hji,hjv->hiv", state_map, held, precision=highest_precision)


def mat_nt(first_mat, second_mat):
    return lax.dot_general(
        first_mat, second_mat, (((1,), (1,)), ((), ())), preferred_element_type=jnp.float32
    )


def mat_tn(first_mat, second_mat):
    return lax.dot_general(
        first_mat, second_mat, (((0,), (0,)), ((), ())), preferred_element_type=jnp.float32
    )


def mat_nn(first_mat, second_mat):
    return jnp.dot(first_mat, second_mat, preferred_element_type=jnp.float32)


def rms_scale(hidden, gain_vec):
    return (
        hidden * lax.rsqrt(jnp.mean(hidden * hidden, axis=-1, keepdims=True) + epsilon) * gain_vec
    )


def swiglu(gate_part, up_part):
    return jax.nn.silu(gate_part) * up_part


def short_conv(padded, conv_all):
    length = padded.shape[0] - (KW - 1)
    mixed_rows = padded[0:length] * conv_all[0]
    for tap_index in range(1, KW):
        mixed_rows = mixed_rows + padded[tap_index : tap_index + length] * conv_all[tap_index]
    return mixed_rows


def decay_rates(rates, decay_log, decay_bias):
    heads = decay_log.shape[0]
    pairs = jnp.transpose(rates.reshape(rates.shape[0], heads, 2), (2, 1, 0))
    log_decay = -jnp.exp(decay_log)[:, None] * jax.nn.softplus(pairs[0] + decay_bias[:, None])
    strength = jax.nn.sigmoid(pairs[1])
    return log_decay[:, :, None], strength[:, :, None]


def split_columns(matrix, widths):
    pieces = []
    offset_col = 0
    for width_one in widths:
        pieces.append(matrix[:, offset_col : offset_col + width_one])
        offset_col = offset_col + width_one
    return pieces


def head_halves(weights, parts):
    slabs = []
    for part in range(parts):
        cut = []
        for weight in weights:
            width = weight.shape[1] // parts
            cut.append(weight[:, part * width : (part + 1) * width])
        slabs.append(jnp.concatenate(cut, axis=1))
    return jnp.stack(slabs)


def swap_halves(slabs):
    if slabs.shape[0] == 2:
        me = lax.axis_index("head")
        sent = lax.dynamic_index_in_dim(slabs, 1 - me, 0, keepdims=False)
        kept = lax.dynamic_index_in_dim(slabs, me, 0, keepdims=False)
        moved = lax.ppermute(sent, "head", [(0, 1), (1, 0)])
        return jnp.where(me == 0, jnp.stack([kept, moved]), jnp.stack([moved, kept]))
    return lax.all_to_all(slabs, "head", split_axis=0, concat_axis=0, tiled=True)


def whole_rows(slabs):
    full = lax.all_gather(slabs, ("ctx", "batch"), axis=1, tiled=True)
    return full.reshape(full.shape[0] * full.shape[1], full.shape[2])


def other_parts(block):
    parts = lax.axis_size("head")
    total = None
    for shift in range(1, parts):
        moved = lax.ppermute(block, "head", [(i, (i + shift) % parts) for i in range(parts)])
        moved = moved.astype(jnp.float32)
        total = moved if total is None else total + moved
    return total


def head_sum(partial, kind=jnp.bfloat16):
    sent = partial.astype(kind)
    if lax.axis_size("head") == 1:
        return sent.astype(jnp.float32)
    return sent.astype(jnp.float32) + other_parts(sent)


def own_rows_sum(partial):
    parts = lax.axis_size("head")
    rows = partial.shape[0] // parts
    me = lax.axis_index("head")
    total = lax.dynamic_slice_in_dim(partial, me * rows, rows, 0)
    for shift in range(1, parts):
        target = lax.rem(me + shift, parts)
        sent = lax.dynamic_slice_in_dim(partial, target * rows, rows, 0).astype(jnp.bfloat16)
        route = [(i, (i + shift) % parts) for i in range(parts)]
        total = total + lax.ppermute(sent, "head", route).astype(jnp.float32)
    return total


MESH_ID = pl.DeviceIdType.MESH
PAIR = 2


def staged(rows):
    parts = lax.axis_size("ctx") * lax.axis_size("batch")
    return lax.axis_size("batch") == 2 * PAIR and rows % parts == 0 and (rows // parts) % 16 == 0


def places():
    c = lax.axis_index("ctx")
    b = lax.axis_index("batch")
    k = lax.rem(b, PAIR)
    x = lax.div(b, PAIR)
    return c, x, k, x * PAIR + (1 - k), (1 - x) * PAIR + k


def greet(n, partner, across, c, facing=None):
    barrier = pltpu.get_barrier_semaphore()
    count = n + 1
    if facing is not None:
        pl.semaphore_signal(barrier, inc=1, device_id={"head": facing}, device_id_type=MESH_ID)
        count += 1
    for shift in range(1, n):
        pl.semaphore_signal(
            barrier, inc=1, device_id={"ctx": lax.rem(c + shift, n)}, device_id_type=MESH_ID
        )
    for other in (partner, across):
        pl.semaphore_signal(barrier, inc=1, device_id={"batch": other}, device_id_type=MESH_ID)
    pl.semaphore_wait(barrier, count)


def scatter_kernel(
    n, steps, widths, a_ref, sm_ref, *refs
):
    outs = refs[: len(widths)]
    (
        sm_out, from_pair, paired, from_across, held, from_left, from_right, acc,
        sm_in, sm_sent, sm_all,
        pair_send, pair_recv, cross_send, cross_recv, line_send, left_recv, right_recv,
        sm_send, sm_recv, all_send, all_recv,
    ) = refs[len(widths) :]
    c, x, k, partner, across = places()
    right = jnp.minimum(c + 1, n - 1)
    left = jnp.maximum(c - 1, 0)
    greet(n, partner, across, c)

    def to_pair(q):
        return pltpu.make_async_remote_copy(
            a_ref.at[:, :, 1 - k, q], from_pair.at[q], pair_send.at[q], pair_recv.at[q],
            device_id={"batch": partner}, device_id_type=MESH_ID,
        )

    def to_across(q):
        return pltpu.make_async_remote_copy(
            paired.at[q, 1 - x], from_across.at[q], cross_send.at[q], cross_recv.at[q],
            device_id={"batch": across}, device_id_type=MESH_ID,
        )

    def to_right(q, at):
        return pltpu.make_async_remote_copy(
            held.at[q, at], from_left.at[q, at], line_send.at[q, at], left_recv.at[q, at],
            device_id={"ctx": right}, device_id_type=MESH_ID,
        )

    def to_left(q, at):
        return pltpu.make_async_remote_copy(
            held.at[q, at], from_right.at[q, at], line_send.at[q, at], right_recv.at[q, at],
            device_id={"ctx": left}, device_id_type=MESH_ID,
        )

    def small(source, stage, other):
        return pltpu.make_async_remote_copy(
            source, sm_in.at[stage], sm_send.at[stage], sm_recv.at[stage],
            device_id={"batch": other}, device_id_type=MESH_ID,
        )

    def small_all(shift):
        peer = lax.rem(c + shift, n)
        return pltpu.make_async_remote_copy(
            sm_sent.at[1], sm_all.at[c], all_send.at[shift], all_recv.at[n - shift],
            device_id={"ctx": peer}, device_id_type=MESH_ID,
        )

    def small_from(shift):
        peer = lax.rem(c + shift, n)
        return pltpu.make_async_remote_copy(
            sm_sent.at[1], sm_all.at[peer], all_send.at[shift], all_recv.at[shift],
            device_id={"ctx": peer}, device_id_type=MESH_ID,
        )

    def begin(q, carry):
        to_pair(q).start()
        return carry

    lax.fori_loop(0, steps, begin, 0)
    first_small = small(sm_ref, 0, partner)
    first_small.start()

    def pair_up(q, carry):
        to_pair(q).wait_recv()

        def add(at, inner):
            for side in range(2):
                total = a_ref[at, side, k, q].astype(jnp.float32) + from_pair[
                    q, at, side
                ].astype(jnp.float32)
                paired[q, side, at] = total.astype(jnp.bfloat16)
            return inner

        lax.fori_loop(0, n, add, 0)
        to_across(q).start()
        return carry

    lax.fori_loop(0, steps, pair_up, 0)
    first_small.wait()
    sm_sent[0] = sm_ref[...] + sm_in[0]
    second_small = small(sm_sent.at[0], 1, across)
    second_small.start()

    def cross_up(q):
        to_across(q).wait_recv()

        def add(at, inner):
            total = paired[q, x, at].astype(jnp.float32) + from_across[q, at].astype(jnp.float32)
            held[q, at] = total.astype(jnp.bfloat16)
            return inner

        lax.fori_loop(0, n, add, 0)

        @pl.when(c == 0)
        def _():
            for at in range(n - 1, 0, -1):
                to_right(q, at).start()

        @pl.when(c == n - 1)
        def _():
            for at in range(n - 1):
                to_left(q, at).start()

    def relay(hop, q):
        @pl.when(c == hop)
        def _():
            for at in range(n - 1, hop, -1):
                to_right(q, at).wait_recv()
                total = held[q, at].astype(jnp.float32) + from_left[q, at].astype(jnp.float32)
                held[q, at] = total.astype(jnp.bfloat16)
                to_right(q, at).start()

        @pl.when(c == n - 1 - hop)
        def _():
            for at in range(n - 1 - hop):
                to_left(q, at).wait_recv()
                total = held[q, at].astype(jnp.float32) + from_right[q, at].astype(jnp.float32)
                held[q, at] = total.astype(jnp.bfloat16)
                to_left(q, at).start()

    def finish(q):
        acc[...] = paired[q, x, c].astype(jnp.float32) + from_across[q, c].astype(jnp.float32)

        @pl.when(c > 0)
        def _():
            to_right(q, c).wait_recv()
            acc[...] += from_left[q, c].astype(jnp.float32)

        @pl.when(c < n - 1)
        def _():
            to_left(q, c).wait_recv()
            acc[...] += from_right[q, c].astype(jnp.float32)

        first = 0
        for out, width in zip(outs, widths):
            out[q] = acc[:, first : first + width]
            first += width

    second_small.wait()
    sm_sent[1] = sm_sent[0] + sm_in[1]
    for shift in range(1, n):
        small_all(shift).start()

    def beat(tick, carry):
        @pl.when(tick < steps)
        def _():
            cross_up(tick)

        for hop in range(1, n - 1):
            q = tick - hop

            @pl.when((q >= 0) & (q < steps))
            def _():
                relay(hop, q)

        last = tick - (n - 1)

        @pl.when(last >= 0)
        def _():
            finish(last)

        return carry

    lax.fori_loop(0, steps + n - 1, beat, 0)
    sm_all[c] = sm_sent[1]
    for shift in range(1, n):
        small_from(shift).wait_recv()
        small_all(shift).wait_send()
    total = sm_all[0]
    for at in range(1, n):
        total = total + sm_all[at]
    sm_out[...] = total

    def drain(q, carry):
        to_pair(q).wait_send()
        to_across(q).wait_send()

        def line(at, inner):
            @pl.when(at > c)
            def _():
                to_right(q, at).wait_send()

            @pl.when(at < c)
            def _():
                to_left(q, at).wait_send()

            return inner

        lax.fori_loop(0, n, line, 0)
        return carry

    lax.fori_loop(0, steps, drain, 0)


def scatter_sum(products, smalls, widths):
    n = lax.axis_size("ctx")
    parts = n * lax.axis_size("batch")
    rows = products.shape[0] // parts
    cols = products.shape[1]
    steps = rows // 16
    blocks = products.reshape(n, 2, 2, steps, 16, cols)
    count = smalls.shape[0]
    lanes = pl.cdiv(count, 1024) * 8
    flat = jnp.pad(smalls, (0, lanes * 128 - count)).reshape(lanes, 128)
    vmem = pl.BlockSpec(memory_space=pltpu.VMEM)
    half = jnp.bfloat16
    dma = pltpu.SemaphoreType.DMA
    results = pl.pallas_call(
        functools.partial(scatter_kernel, n, steps, widths),
        in_specs=[vmem, vmem],
        out_specs=[vmem] * (len(widths) + 1),
        out_shape=[of_shape((steps, 16, width)) for width in widths] + [of_shape(flat.shape)],
        scratch_shapes=[
            pltpu.VMEM((steps, n, 2, 16, cols), half),
            pltpu.VMEM((steps, 2, n, 16, cols), half),
            pltpu.VMEM((steps, n, 16, cols), half),
            pltpu.VMEM((steps, n, 16, cols), half),
            pltpu.VMEM((steps, n, 16, cols), half),
            pltpu.VMEM((steps, n, 16, cols), half),
            pltpu.VMEM((16, cols), jnp.float32),
            pltpu.VMEM((2,) + flat.shape, jnp.float32),
            pltpu.VMEM((2,) + flat.shape, jnp.float32),
            pltpu.VMEM((n,) + flat.shape, jnp.float32),
            dma((steps,)), dma((steps,)), dma((steps,)), dma((steps,)),
            dma((steps, n)), dma((steps, n)), dma((steps, n)),
            dma((2,)), dma((2,)), dma((n,)), dma((n,)),
        ],
        compiler_params=pltpu.CompilerParams(collective_id=0, has_side_effects=True),
        cost_estimate=pl.CostEstimate(
            flops=0, bytes_accessed=4 * products.size * 2, transcendentals=0
        ),
    )(blocks, flat)
    sums = [result.reshape(rows, width) for result, width in zip(results, widths)]
    return sums, results[-1].reshape(-1)[:count]


def gather_kernel(n, slab_ref, tok_ref, cot_ref, *refs):
    (
        out, tok_out, cot_out,
        own_sem, side_send, side_recv, line_send, line_recv,
        cross_send, cross_recv, pair_send, pair_recv,
    ) = refs
    c, x, k, partner, across = places()
    me = lax.axis_index("head")
    other = 1 - me
    right = jnp.minimum(c + 1, n - 1)
    left = jnp.maximum(c - 1, 0)
    greet(n, partner, across, c, other)

    def copy(source, target, send, recv, axis, to):
        return pltpu.make_async_remote_copy(
            source, target, send, recv, device_id={axis: to}, device_id_type=MESH_ID
        )

    def piece(j, at, side, core):
        return out.at[me if j == 0 else other, at, side, core]

    def to_line(j, at, to, source=None):
        spot = piece(j, at, x, k)
        return copy(
            spot if source is None else source, spot,
            line_send.at[j, at], line_recv.at[j, at], "ctx", to,
        )

    def to_across(j, at, side, source=None):
        spot = piece(j, at, side, k)
        return copy(
            spot if source is None else source, spot,
            cross_send.at[j, at], cross_recv.at[j, at], "batch", across,
        )

    def to_pair(j, at, side, core, source=None):
        spot = piece(j, at, side, core)
        return copy(
            spot if source is None else source, spot,
            pair_send.at[j, at, side], pair_recv.at[j, at, side], "batch", partner,
        )

    swap = copy(
        slab_ref.at[other], out.at[me, c, x, k], side_send.at[0], side_recv.at[0], "head", other
    )
    tok_swap = copy(tok_ref, tok_out.at[me], side_send.at[1], side_recv.at[1], "head", other)
    cot_swap = copy(cot_ref, cot_out.at[me], side_send.at[2], side_recv.at[2], "head", other)
    swap.start()

    def own(j, source):
        to_across(j, c, x, source).start()

        @pl.when(c < n - 1)
        def _():
            copy(
                source, piece(j, c, x, k), own_sem.at[3 + j], line_recv.at[j, c], "ctx", right
            ).start()

        @pl.when(c > 0)
        def _():
            copy(
                source, piece(j, c, x, k), own_sem.at[5 + j], line_recv.at[j, c], "ctx", left
            ).start()

        to_pair(j, c, x, k, source).start()

    kept = slab_ref.at[me]
    own(0, kept)
    locals_ = (
        pltpu.make_async_copy(kept, out.at[me, c, x, k], own_sem.at[0]),
        pltpu.make_async_copy(tok_ref, tok_out.at[me], own_sem.at[1]),
        pltpu.make_async_copy(cot_ref, cot_out.at[me], own_sem.at[2]),
    )
    for one in locals_:
        one.start()
    from_side = copy(
        slab_ref.at[other], out.at[other, c, x, k], side_send.at[0], side_recv.at[0], "head", other
    )
    from_side.wait_recv()
    own(1, piece(1, c, x, k))
    tok_swap.start()
    cot_swap.start()

    def cross_done(j, at):
        to_across(j, at, 1 - x).wait_recv()
        to_pair(j, at, 1 - x, k).start()

    for distance in range(1, n + 1):
        for j in range(2):
            for sign in (-1, 1):
                at = c + sign * distance
                back = c + sign * (distance - 1)
                onward = right if sign < 0 else left
                more = (c < n - 1) if sign < 0 else (c > 0)
                if distance < n:

                    @pl.when((at >= 0) & (at < n))
                    def _():
                        to_line(j, at, onward).wait_recv()

                        @pl.when(more)
                        def _():
                            to_line(j, at, onward).start()

                        to_across(j, at, x).start()
                        to_pair(j, at, x, k).start()

                if distance > 1:

                    @pl.when((back >= 0) & (back < n))
                    def _():
                        cross_done(j, back)

                elif sign < 0:
                    cross_done(j, c)

    for j in range(2):

        def settle(at, carry):
            for side in range(2):
                to_pair(j, at, side, 1 - k).wait_recv()
                to_pair(j, at, side, k).wait_send()
            to_across(j, at, x).wait_send()

            @pl.when(((at < c) & (c < n - 1)) | ((at > c) & (c > 0)))
            def _():
                to_line(j, at, right).wait_send()

            return carry

        lax.fori_loop(0, n, settle, 0)
        spot = piece(j, c, x, k)

        @pl.when(c < n - 1)
        def _():
            copy(spot, spot, own_sem.at[3 + j], line_recv.at[j, c], "ctx", right).wait_send()

        @pl.when(c > 0)
        def _():
            copy(spot, spot, own_sem.at[5 + j], line_recv.at[j, c], "ctx", left).wait_send()

    for one in locals_:
        one.wait()
    swap.wait_send()
    for sent, target, slot in ((tok_swap, tok_out, 1), (cot_swap, cot_out, 2)):
        sent.wait_send()
        copy(
            target.at[other], target.at[other], side_send.at[slot], side_recv.at[slot], "head", other
        ).wait_recv()


def gathers(slabs):
    return (
        lax.axis_size("head") == 2
        and lax.axis_size("batch") == 2 * PAIR
        and slabs.shape[1] % 16 == 0
    )


def gather_all(slabs, tok, cot):
    n = lax.axis_size("ctx")
    rows, cols = slabs.shape[1:]
    vmem = pl.BlockSpec(memory_space=pltpu.VMEM)
    anywhere = pl.BlockSpec(memory_space=pl.ANY)
    dma = pltpu.SemaphoreType.DMA
    half = jnp.bfloat16
    weight, tokens, cots = pl.pallas_call(
        functools.partial(gather_kernel, n),
        in_specs=[vmem] * 3,
        out_specs=[anywhere] * 3,
        out_shape=[
            of_shape((2, n, 2, 2, rows, cols), half),
            of_shape((2,) + tok.shape, half),
            of_shape((2,) + cot.shape, half),
        ],
        scratch_shapes=[
            dma((7,)), dma((3,)), dma((3,)), dma((2, n)), dma((2, n)),
            dma((2, n)), dma((2, n)), dma((2, n, 2)), dma((2, n, 2)),
        ],
        compiler_params=pltpu.CompilerParams(collective_id=1, has_side_effects=True),
        cost_estimate=pl.CostEstimate(
            flops=0, bytes_accessed=64 * n * rows * cols, transcendentals=0
        ),
    )(slabs, tok, cot)
    return (
        weight.reshape(8 * n * rows, cols),
        tokens.reshape(-1, tok.shape[1]),
        cots.reshape(-1, cot.shape[1]),
    )


def outer_kernel(*refs):
    out = refs[-1]
    first = 0
    for left_ref, right_ref in zip(refs[:-1:2], refs[1:-1:2]):
        width = right_ref.shape[1]
        part = one_pass(left_ref[...], right_ref[...], 0, 0)
        out[:, first : first + width] = part.astype(out.dtype)
        first += width


def outer_products(*pairs):
    tokens, features = pairs[0][0].shape
    block = min(256, features)
    total = sum(second.shape[1] for _, second in pairs)
    specs = []
    for _, second in pairs:
        specs.append(pl.BlockSpec((tokens, block), lambda i: (0, i)))
        specs.append(pl.BlockSpec(second.shape, lambda i: (0, 0)))
    args = [one for pair in pairs for one in pair]
    return pl.pallas_call(
        outer_kernel,
        grid=(features // block,),
        in_specs=specs,
        out_specs=pl.BlockSpec((block, total), lambda i: (i, 0)),
        out_shape=of_shape((features, total), jnp.bfloat16),
        cost_estimate=pl.CostEstimate(
            flops=2 * tokens * features * total,
            bytes_accessed=2 * features * total,
            transcendentals=0,
        ),
    )(*args)


def chain_kernel(n, forward, map_ref, offset_ref, state_ref, sent, landed, send_sem, recv_sem):
    c = lax.axis_index("ctx")
    heads = map_ref.shape[0]
    place = c if forward else n - 1 - c
    ahead = jnp.minimum(c + 1, n - 1) if forward else jnp.maximum(c - 1, 0)
    behind = jnp.maximum(c - 1, 0) if forward else jnp.minimum(c + 1, n - 1)
    barrier = pltpu.get_barrier_semaphore()

    @pl.when(place > 0)
    def _():
        pl.semaphore_signal(barrier, inc=1, device_id={"ctx": behind}, device_id_type=MESH_ID)

    @pl.when(place < n - 1)
    def _():
        pl.semaphore_wait(barrier, 1)

    def pass_on(head):
        return pltpu.make_async_remote_copy(
            sent.at[head], landed.at[head], send_sem.at[head], recv_sem.at[head],
            device_id={"ctx": ahead}, device_id_type=MESH_ID,
        )

    @pl.when(place == 0)
    def _():
        sent[...] = offset_ref[...].astype(jnp.bfloat16)
        for head in range(heads):
            pass_on(head).start()
        state_ref[...] = jnp.zeros_like(state_ref)

    @pl.when(place > 0)
    def _():
        for head in range(heads):
            pass_on(head).wait_recv()
            start = landed[head].astype(jnp.float32)

            @pl.when(place < n - 1)
            def _():
                moved = offset_ref[head] + product(
                    map_ref[head], start, 1 if forward else 0, 0
                )
                sent[head] = moved.astype(jnp.bfloat16)
                pass_on(head).start()

            state_ref[head] = start

    @pl.when(place < n - 1)
    def _():
        for head in range(heads):
            pass_on(head).wait_send()


def chain(piece_map, piece_offset, forward):
    n = lax.axis_size("ctx")
    heads = piece_map.shape[0]
    vmem = pl.BlockSpec(memory_space=pltpu.VMEM)
    dma = pltpu.SemaphoreType.DMA
    return pl.pallas_call(
        functools.partial(chain_kernel, n, forward),
        in_specs=[vmem, vmem],
        out_specs=vmem,
        out_shape=of_shape(piece_offset.shape),
        scratch_shapes=[
            pltpu.VMEM(piece_offset.shape, jnp.bfloat16),
            pltpu.VMEM(piece_offset.shape, jnp.bfloat16),
            dma((heads,)), dma((heads,)),
        ],
        compiler_params=pltpu.CompilerParams(
            collective_id=2 if forward else 3, has_side_effects=True
        ),
        cost_estimate=pl.CostEstimate(
            flops=0, bytes_accessed=8 * n * piece_offset.size, transcendentals=0
        ),
    )(piece_map, piece_offset)


def body(
    tokens,
    cotangent,
    norm1_gain,
    w_query,
    w_key,
    w_value,
    w_gate,
    w_rates,
    conv_query,
    conv_key,
    conv_value,
    decay_log,
    decay_bias,
    out_gain,
    w_out,
    norm2_gain,
    w_ffgate,
    w_ffup,
    w_down,
):
    parts = lax.axis_size("head")
    me = lax.axis_index("head")
    heads = decay_log.shape[0]
    query_width = conv_query.shape[1]
    value_width = conv_value.shape[1]
    dk = query_width // heads
    dv = value_width // heads
    margin = KW - 1
    gains = jnp.stack([norm1_gain, norm2_gain], axis=1)
    slabs_in = head_halves(
        [w_query, w_key, w_value, w_gate, w_rates, jnp.tile(gains, (1, parts))], parts
    )
    rates_width = w_rates.shape[1] // parts
    mixed_width = 2 * query_width + value_width
    proj_width = mixed_width + value_width + rates_width
    later = swap_halves(head_halves([w_out, w_ffgate, w_ffup, w_down], parts))
    ff_local = w_down.shape[1] // parts
    if gathers(slabs_in):
        later, slabs_in = lax.optimization_barrier((later, slabs_in))
        later_weight = whole_rows(later)
        in_weight, piece_tok, cot = gather_all(slabs_in, tokens[0], cotangent[0])
    else:
        in_weight = whole_rows(swap_halves(slabs_in))
        later_weight = whole_rows(later)
        piece_tok = lax.all_gather(tokens[0], "head", axis=0, tiled=True)
        cot = lax.all_gather(cotangent[0], "head", axis=0, tiled=True)
    gain_cols = in_weight[:, proj_width:].astype(jnp.float32)
    gain_one = gain_cols[:, 0]
    gain_two = gain_cols[:, 1]
    out_weight = later_weight[:, :value_width]
    ff_weight = later_weight[:, value_width : value_width + 2 * ff_local]
    down_weight = later_weight[:, value_width + 2 * ff_local :]

    inputs_tok = tokens[0]
    own_count = inputs_tok.shape[0]
    residual = piece_tok.astype(jnp.float32)
    piece_rows = residual.shape[0]
    normed_one = rms_scale(residual, gain_one).astype(jnp.bfloat16)
    proj = mat_nn(normed_one, in_weight[:, :proj_width]).astype(jnp.bfloat16)
    joined = proj[:, :mixed_width]
    rates_here = proj[:, mixed_width + value_width :]
    rim_rows = passed_along(joined[piece_rows - margin :], "ctx", 1)
    padded = jnp.concatenate([rim_rows, joined], axis=0).astype(jnp.float32)
    conv_all = jnp.concatenate([conv_query, conv_key, conv_value], axis=1).astype(jnp.float32)
    mixed, conv_vjp = jax.vjp(short_conv, padded, conv_all)
    (log_decay, strength), rates_vjp = jax.vjp(
        decay_rates, rates_here.astype(jnp.float32), decay_log, decay_bias
    )
    value_first = 2 * query_width // dv
    chunk = min(CHUNK, piece_rows)
    chunks = piece_rows // chunk
    grid = (heads, chunks)
    log_decay = log_decay.reshape(heads, chunks, chunk, 1)
    strength = strength.reshape(heads, chunks, chunk, 1)
    mixed_specs = [
        columns(chunk, dk, 0),
        columns(chunk, dk, heads),
        columns(chunk, dv, value_first),
        heads_spec(chunk, 1),
        heads_spec(chunk, 1),
    ]
    square = heads_spec(chunk, chunk)
    state = heads_spec(dk, dv)
    rows_v = columns(chunk, dv, 0)
    rows_k = columns(chunk, dk, 0)
    inverse, local_out, effect, state_map, state_offset = per_head(
        forward_kernel,
        grid,
        mixed_specs,
        [
            (square, of_shape((heads, chunks, chunk, chunk))),
            (rows_v, of_shape((piece_rows, value_width))),
            (rows_k, of_shape((piece_rows, query_width))),
            (heads_spec(dk, dk), of_shape((heads, chunks, dk, dk))),
            (state, of_shape((heads, chunks, dk, dv))),
        ],
        (mixed, mixed, mixed, log_decay, strength),
        heads * 100 * piece_rows * chunk**2,
    )
    chunk_maps = [state_map[:, i] for i in range(chunks)]
    chunk_offsets = [state_offset[:, i] for i in range(chunks)]
    piece_map = chunk_maps[0]
    piece_offset = chunk_offsets[0]
    for i in range(1, chunks):
        piece_map = state_product(chunk_maps[i], piece_map)
        piece_offset = state_product(chunk_maps[i], piece_offset) + chunk_offsets[i]
    start_state = chain(piece_map, piece_offset, True)
    starts = [start_state]
    for i in range(1, chunks):
        starts.append(state_product(chunk_maps[i - 1], starts[-1]) + chunk_offsets[i - 1])
    start_states = jnp.stack(starts, axis=1)
    gain_row = out_gain.astype(jnp.float32)[None]
    gate_spec = columns(chunk, dv, mixed_width // dv)
    gain_spec = pl.BlockSpec((1, dv), lambda h, c: (0, h))
    gain_out = pl.BlockSpec((None, 1, dv), lambda h, c: (c, 0, h))
    gate_ins = [rows_v, rows_k, state, gate_spec, gain_spec]
    gate_args = (local_out, effect, start_states, proj, gain_row)
    (gated,) = per_head(
        gate_kernel,
        grid,
        gate_ins,
        [(rows_v, of_shape((piece_rows, value_width), jnp.bfloat16))],
        gate_args,
        heads * 12 * piece_rows * dk * dv,
    )
    middle = residual + head_sum(mat_nt(gated, out_weight))
    normed_two_f, norm_two_vjp = jax.vjp(rms_scale, middle, gain_two)
    normed_two = normed_two_f.astype(jnp.bfloat16)
    ff_both = mat_nn(normed_two, ff_weight)
    hidden_f, swiglu_vjp = jax.vjp(swiglu, ff_both[:, :ff_local], ff_both[:, ff_local:])
    hidden = hidden_f.astype(jnp.bfloat16)
    hidden_grad = mat_nn(cot, down_weight)
    gate_grad_f, up_grad_f = swiglu_vjp(hidden_grad)
    ff_grads = jnp.concatenate([gate_grad_f, up_grad_f], axis=1).astype(jnp.bfloat16)
    middle_part, gain_two_grad = norm_two_vjp(head_sum(mat_nt(ff_grads, ff_weight)))
    middle_grad = cot.astype(jnp.float32) + middle_part
    middle_grad_b = middle_grad.astype(jnp.bfloat16)
    gated_grad = mat_nn(middle_grad_b, out_weight).astype(jnp.bfloat16)
    middle_own = lax.dynamic_slice_in_dim(middle, me * own_count, own_count, 0)
    output_tok = (middle_own + own_rows_sum(mat_nt(hidden, down_weight))).astype(jnp.bfloat16)

    mixer_grad, gate_bf, out_gain_grad, reach = per_head(
        gate_back_kernel,
        grid,
        gate_ins + [rows_v],
        [
            (rows_v, of_shape((piece_rows, value_width))),
            (rows_v, of_shape((piece_rows, value_width), jnp.bfloat16)),
            (gain_out, of_shape((chunks, 1, value_width))),
            (state, of_shape((heads, chunks, dk, dv))),
        ],
        gate_args + (gated_grad,),
        heads * 24 * piece_rows * dk * dv,
    )
    chunk_reach = [reach[:, i] for i in range(chunks)]
    piece_reach = chunk_reach[chunks - 1]
    for i in range(chunks - 2, -1, -1):
        piece_reach = chunk_reach[i] + state_pull(chunk_maps[i], piece_reach)
    last_grad = chain(piece_map, piece_reach, False)
    lasts = [last_grad]
    for i in range(chunks - 1, 0, -1):
        lasts.insert(0, chunk_reach[i] + state_pull(chunk_maps[i], lasts[0]))
    last_grads = jnp.stack(lasts, axis=1)

    ff_products = outer_products(
        (middle_grad_b, gated), (normed_two, ff_grads), (cot, hidden)
    )
    ff_sums = lax.psum_scatter(
        ff_products,
        ("ctx", "batch"),
        scatter_dimension=0,
        tiled=True,
    )

    query_g, key_g, value_g, decay_g, strength_g = per_head(
        backward_kernel,
        grid,
        mixed_specs + [square, state, rows_v, state],
        [
            (rows_k, of_shape((piece_rows, query_width))),
            (rows_k, of_shape((piece_rows, query_width))),
            (rows_v, of_shape((piece_rows, value_width))),
            (heads_spec(chunk, 1), of_shape((heads, chunks, chunk, 1))),
            (heads_spec(chunk, 1), of_shape((heads, chunks, chunk, 1))),
        ],
        (mixed, mixed, mixed, log_decay, strength, inverse, start_states, mixer_grad, last_grads),
        heads * 100 * piece_rows * chunk**2,
    )
    padded_grad, conv_grad = conv_vjp(jnp.concatenate([query_g, key_g, value_g], axis=1))
    rates_grad_f, decay_log_grad, decay_bias_grad = rates_vjp(
        (decay_g.reshape(heads, piece_rows, 1), strength_g.reshape(heads, piece_rows, 1))
    )
    back_rim = passed_along(padded_grad[:margin], "ctx", -1)
    own_rows = padded_grad[margin:]
    own_rows = jnp.concatenate(
        [own_rows[: piece_rows - margin], own_rows[piece_rows - margin :] + back_rim], axis=0
    ).astype(jnp.bfloat16)
    proj_grad = jnp.concatenate([own_rows, gate_bf, rates_grad_f.astype(jnp.bfloat16)], axis=1)
    proj_products = outer_products((normed_one, proj_grad))
    own_grad = own_rows_sum(mat_nt(proj_grad, in_weight[:, :proj_width]))
    unused_rows, norm_one_vjp = jax.vjp(rms_scale, inputs_tok.astype(jnp.float32), gain_one)
    input_part, gain_one_grad = norm_one_vjp(own_grad)
    input_grad = lax.dynamic_slice_in_dim(middle_grad, me * own_count, own_count, 0) + input_part
    smalls = (
        conv_grad.reshape(-1),
        jnp.sum(out_gain_grad, axis=(0, 1)),
        head_sum(gain_one_grad, jnp.float32),
        gain_two_grad,
        decay_log_grad,
        decay_bias_grad,
    )
    proj_widths = (query_width, query_width, value_width, value_width, rates_width)
    if staged(proj_products.shape[0]):
        proj_parts, summed = scatter_sum(proj_products, jnp.concatenate(smalls), proj_widths)
    else:
        proj_sums = lax.psum_scatter(
            proj_products, ("ctx", "batch"), scatter_dimension=0, tiled=True
        ).astype(jnp.float32)
        proj_parts = split_columns(proj_sums, proj_widths)
        summed = lax.psum(jnp.concatenate(smalls), ("ctx", "batch"))
    ff_parts = split_columns(
        ff_sums.astype(jnp.float32), (value_width, ff_local, ff_local, ff_local)
    )
    cuts = []
    first = 0
    for small in smalls:
        cuts.append(summed[first : first + small.shape[0]])
        first += small.shape[0]
    conv_sum = cuts[0].reshape(conv_grad.shape)
    share = norm1_gain.shape[0]
    place = (me * lax.axis_size("ctx") + lax.axis_index("ctx")) * lax.axis_size("batch")
    place = (place + lax.axis_index("batch")) * share
    return (
        output_tok[None],
        input_grad[None],
        lax.dynamic_slice_in_dim(cuts[2], place, share, 0),
        proj_parts[0],
        proj_parts[1],
        proj_parts[2],
        proj_parts[3],
        proj_parts[4],
        conv_sum[:, :query_width],
        conv_sum[:, query_width : 2 * query_width],
        conv_sum[:, 2 * query_width :],
        cuts[4],
        cuts[5],
        cuts[1],
        ff_parts[0],
        lax.dynamic_slice_in_dim(cuts[3], place, share, 0),
        ff_parts[1],
        ff_parts[2],
        ff_parts[3],
    )


def solution(mesh):
    placed = (
        P("batch", ("ctx", "head"), None),
        P("batch", ("ctx", "head"), None),
        P(("head", "ctx", "batch")),
        P(("head", "ctx", "batch"), None),
        P(("head", "ctx", "batch"), None),
        P(("head", "ctx", "batch"), None),
        P(("head", "ctx", "batch"), None),
        P(("head", "ctx", "batch"), None),
        P(None, "head"),
        P(None, "head"),
        P(None, "head"),
        P("head"),
        P("head"),
        P("head"),
        P(("head", "ctx", "batch"), None),
        P(("head", "ctx", "batch")),
        P(("head", "ctx", "batch"), None),
        P(("head", "ctx", "batch"), None),
        P(("head", "ctx", "batch"), None),
    )
    return jax.shard_map(
        body,
        mesh=mesh,
        in_specs=placed,
        out_specs=(
            P("batch", ("ctx", "head"), None),
            P("batch", ("ctx", "head"), None),
            P(("head", "ctx", "batch")),
            P(("ctx", "batch"), "head"),
            P(("ctx", "batch"), "head"),
            P(("ctx", "batch"), "head"),
            P(("ctx", "batch"), "head"),
            P(("ctx", "batch"), "head"),
            P(None, "head"),
            P(None, "head"),
            P(None, "head"),
            P("head"),
            P("head"),
            P("head"),
            P(("ctx", "batch"), "head"),
            P(("head", "ctx", "batch")),
            P(("ctx", "batch"), "head"),
            P(("ctx", "batch"), "head"),
            P(("ctx", "batch"), "head"),
        ),
        check_vma=False,
    )
```
